32 devices in a mesh: region: 4 (over y, x), scen: 8 (over z, core).
Axes of the slice: x: 2, y: 2, z: 4, core: 2. Of those that a mesh axis runs over, the one named last changes fastest.
Arguments:
- start_state: float32 [4, 128, 24, 1024], P('region', 'scen'), may hold values from -6 to 6
- price: float32 [4, 128, 24, 1024], P('region', 'scen'), may hold values from -6 to 6
- demand: float32 [4, 128, 24, 1024], P('region', 'scen'), may hold values from 0.2 to 2
- sens: bfloat16 [4, 1024, 1024], P('region'), as said below
- gen_bus: int32 [4, 512], P('region'), may hold values from 0 to 1023
- gen_cap: float32 [4, 512], P('region'), may hold values from 0.5 to 3
- tie_index: int32 [4, 2, 512], P('region'), may hold values from 0 to 1023, as said below
- tie_len: int32 [4, 2], P('region'), may hold values from 128 to 512, as said below
Outputs:
- final_state: float32 [4, 128, 24, 1024], P('region', 'scen')
- plan: float32 [4, 24, 1024], P('region')
The draws below stay inside these ranges and needn't reach their ends.
Inputs may be any that keep to these rules, and one draw needn't show every extreme that they name: `tie_index`: for each region the two rows together hold each of the 1024 bus numbers exactly once. tie_len[r, 1] equals tie_len[(r + 1) mod 4, 0]; some border has exactly 512 live slots. `sens`: each matrix has a positive diagonal between 0.5 and 2 and off-diagonal entries of order 1 / sqrt(1024).
All inputs are finite; a program needn't handle non-finite values.
Results may differ from the reference program's by a relative error of at most 0.00098.
Values sent between devices are 32-bit elements; how exact they have to be, the bound alone decides.
A program may use at most 64 MiB of HBM per device.

```python
import math
import jax
import jax.numpy as jnp
from jax import lax

NB = 1024
TIE = 512
H = 24
G = 512
SWEEPS = 2
STEPS = 3
REGIONS = 4
SCEN = 128


def draw_sens(key, part):
    key_diag, key_off = jax.random.split(key, 2)
    diagonal = jnp.exp(jax.random.uniform(key_diag, (REGIONS, NB), jnp.float32, math.log(0.5), math.log(2.0)))
    off_part = jax.random.normal(key_off, (REGIONS, NB, NB), jnp.float32) * 0.5 / NB ** 0.5
    identity = jnp.eye(NB, dtype=jnp.float32)
    return (off_part * (1.0 - identity) + diagonal[:, :, None] * identity).astype(jnp.bfloat16)


def draw_tie_index(key, part):
    region_keys = jax.random.split(key, REGIONS)

    def one_region(region_key):
        return jax.random.permutation(region_key, NB).reshape(2, NB // 2)
    return jax.vmap(one_region)(region_keys).astype(jnp.int32)


def draw_tie_len(key, part):
    key_len, key_place = jax.random.split(key)
    border = jax.random.randint(key_len, (REGIONS,), TIE // 4, TIE + 1)
    chosen = jax.random.randint(key_place, (), 0, REGIONS)
    border = jnp.where(jnp.arange(REGIONS) == chosen, TIE, border)
    return jnp.stack([jnp.roll(border, 1), border], axis=1).astype(jnp.int32)


def set_ends(drawn, stream_key, low, top_value):
    longest = drawn.shape.index(max(drawn.shape))
    spots = []
    for shift in (0, 1):
        where = [jax.random.randint(jax.random.fold_in(stream_key, axis), (), 0, length) for axis, length in enumerate(drawn.shape)]
        where[longest] = (where[longest] + shift) % drawn.shape[longest]
        spots.append(tuple(where))
    return drawn.at[spots[0]].set(low).at[spots[1]].set(top_value)


def block_levels(key, extent, cuts, low, top_value):
    loudness = 1.0
    for position, parts in cuts:
        draws = jax.random.uniform(jax.random.fold_in(jax.random.fold_in(key, 6), position), (parts,), jnp.float32, low / len(cuts), top_value / len(cuts))
        loudness = loudness * jnp.repeat(jnp.exp(draws), extent[position] // parts).reshape((-1,) + (1,) * (len(extent) - 1 - position))
    return loudness


def normal_values(rng, extent, width, limit, pieces=(), kind=jnp.bfloat16):
    array = width * jax.random.normal(rng, extent, jnp.float32)
    if pieces:
        array = array * block_levels(rng, extent, pieces, -0.22, 0.18)
    return jnp.clip(array, -limit, limit).astype(kind)


def setup_inputs(seed: int = 0) -> dict:
    seeds = jax.random.split(jax.random.key(seed), 9)
    start_state = normal_values(seeds[0], (REGIONS, SCEN, H, NB), 1.0, 6.0, ((0, 4), (1, 8)), jnp.float32)
    price = normal_values(seeds[1], (REGIONS, SCEN, H, NB), 1.0, 6.0, ((0, 4), (1, 8)), jnp.float32)
    demand = jnp.clip(jnp.exp(math.log(2.0) - 2.3025851 * jax.random.uniform(seeds[2], (REGIONS, SCEN, H, NB), jnp.float32) ** block_levels(seeds[2], (REGIONS, SCEN, H, NB), ((0, 4), (1, 8)), -0.2, 0.2)), 0.2, 2.0)
    sens = draw_sens(jax.random.fold_in(seeds[8], 71), 0)
    gen_bus = set_ends(jax.random.randint(seeds[4], (REGIONS, G), 0, NB), jax.random.fold_in(seeds[4], 1), 0, NB - 1).astype(jnp.int32)
    gen_cap = jnp.clip(jnp.exp(math.log(3.0) - 1.7917595 * jax.random.uniform(seeds[5], (REGIONS, G), jnp.float32) ** block_levels(seeds[5], (REGIONS, G), ((0, 4),), -0.2, 0.2)), 0.5, 3.0)
    tie_index = draw_tie_index(jax.random.fold_in(seeds[8], 71), 0)
    tie_len = draw_tie_len(jax.random.fold_in(seeds[8], 71), 0)
    return {"start_state": start_state, "price": price, "demand": demand, "sens": sens, "gen_bus": gen_bus, "gen_cap": gen_cap, "tie_index": tie_index, "tie_len": tie_len}


step_rate = 0.3
tie_weight = 1.0
day_weight = 0.5


def pick_blocks(region_state, indices):
    return jnp.stack([region_state[..., indices[0]], region_state[..., indices[1]]])


def place_blocks(values, indices):
    placed = jnp.zeros(values.shape[1:3] + (NB,), jnp.float32)
    placed = placed.at[..., indices[0]].set(values[0])
    return placed.at[..., indices[1]].set(values[1])


def place_mask(live, indices):
    placed = jnp.zeros((NB,), jnp.float32)
    return placed.at[indices[0]].set(live[0]).at[indices[1]].set(live[1])


def add_caps(buses, capacity):
    return jnp.zeros((NB,), jnp.float32).at[buses].add(capacity)


def descend(items):
    state, price_part, demand_part, matrix, target, tie_mask, plan, day_dual, upper = items
    for repeat in range(STEPS):
        rounded = state.reshape(-1, NB).astype(jnp.bfloat16)
        slope = jnp.dot(rounded, matrix, preferred_element_type=jnp.float32).reshape(state.shape)
        slope = slope + price_part + tie_weight * tie_mask * (state - target) + day_weight * (state - plan + day_dual)
        state = jnp.clip(state - step_rate * slope, -demand_part, upper)
    return state


def reference(start_state, price, demand, sens, gen_bus, gen_cap, tie_index, tie_len):
    state = start_state
    live = (jnp.arange(TIE, dtype=jnp.int32)[None, None, :] < tie_len[:, :, None]).astype(jnp.float32)
    upper = jax.vmap(add_caps)(gen_bus, gen_cap)
    tie_mask = jax.vmap(place_mask)(live, tie_index)
    tie_dual = jnp.zeros((REGIONS, 2, SCEN, H, TIE), jnp.float32)
    day_dual = jnp.zeros_like(state)
    plan = jnp.zeros((REGIONS, H, NB), jnp.float32)
    for sweep in range(SWEEPS):
        blocks = jax.vmap(pick_blocks)(state, tie_index)
        from_left = jnp.roll(blocks[:, 1], 1, axis=0)
        from_right = jnp.roll(blocks[:, 0], -1, axis=0)
        theirs = jnp.stack([from_left, from_right], axis=1)
        middle = 0.5 * (blocks + theirs)
        tie_dual = tie_dual + blocks - middle
        target_blocks = (middle - tie_dual) * live[:, :, None, None, :]
        target = jax.vmap(place_blocks)(target_blocks, tie_index)
        plan = jnp.sum(state + day_dual, axis=1) / SCEN
        day_dual = day_dual + state - plan[:, None]
        state = lax.map(descend, (state, price, demand, sens, target, tie_mask, plan, day_dual, upper))
    return state, plan
```

```python
import functools
import jax
import jax.numpy as jnp
from jax import lax
from jax.experimental import pallas as pl
from jax.experimental.pallas import tpu as pltpu
from jax.sharding import PartitionSpec as P

SWEEPS = 2
STEPS = 3
SUB = 8
LANES = 128
TILE = 256
PARTS = 2


step_rate = 0.3
tie_weight = 1.0
day_weight = 0.5

MESH = pl.DeviceIdType.MESH


def kernel(
    total_scen, regions, peers,
    s0_hbm, price_hbm, demand_hbm, sens_hbm, gen_bus_hbm, gen_cap_hbm, tie_index_hbm, tie_len_hbm,
    out, plan_out,
    gen_bus, gen_cap, tie_index, tie_len,
    st, dd, pr, dm, mat, pick, place, mrow, arow, urow, split, rb, kk, first,
    snd, rcv, pbuf,
    token, small_sem, in_sem, mat_sem, send_sem, recv_sem, psend_sem, precv_sem,
):
    chunks, scens, _, buses = st.shape
    slots = tie_index.shape[1]
    rows = scens * SUB
    tiles = buses // TILE
    me = lax.axis_index("scen")
    reg = lax.axis_index("region")
    odd = lax.rem(reg, 2)
    near = reg + 1 - 2 * odd
    far = lax.rem(reg + regions - 1 + 2 * odd, regions)
    square = regions == 4
    across = lax.rem(reg + 2, regions)
    part_rows = rows // PARTS
    part_scens = scens // PARTS

    barrier = pltpu.get_barrier_semaphore()
    for other in (near, across if square else far):
        pl.semaphore_signal(barrier, inc=1, device_id={"region": other}, device_id_type=MESH)
    half = lax.rem(me, 2)
    place_z = lax.div(me, 2)
    last_z = peers // 2 - 1
    lower, higher = {"scen": me - 2}, {"scen": me + 2}
    pl.semaphore_signal(barrier, inc=1, device_id={"scen": me + 1 - 2 * half}, device_id_type=MESH)

    @pl.when(place_z > 0)
    def _():
        pl.semaphore_signal(barrier, inc=1, device_id=lower, device_id_type=MESH)

    @pl.when(place_z < last_z)
    def _():
        pl.semaphore_signal(barrier, inc=1, device_id=higher, device_id_type=MESH)

    def load(kind, source, target, c):
        return pltpu.make_async_copy(source.at[:, pl.ds(pl.multiple_of(c * SUB, SUB), SUB), :], target.at[c], in_sem.at[kind, c])

    def load_first(part):
        some = pl.ds(part * part_scens, part_scens)
        return pltpu.make_async_copy(s0_hbm.at[some, pl.ds(0, SUB), :], st.at[0, some], in_sem.at[0, 0 if part == 0 else chunks - 1 + part])

    small = [
        pltpu.make_async_copy(source, target, small_sem.at[i])
        for i, (source, target) in enumerate((
            (tie_index_hbm, tie_index), (tie_len_hbm, tie_len), (gen_bus_hbm, gen_bus), (gen_cap_hbm, gen_cap),
        ))
    ]
    small[0].start()
    for part in range(PARTS):
        load_first(part).start()
    for c in range(1, chunks):
        load(0, s0_hbm, st, c).start()
    for copy in small[1:]:
        copy.start()

    mat_copy = pltpu.make_async_copy(sens_hbm, mat, mat_sem)
    mat_copy.start()
    for c in range(chunks):
        load(1, price_hbm, pr, c).start()
        load(2, demand_hbm, dm, c).start()

    def one_hot(hit):
        return jnp.where(hit, 1.0, 0.0)

    def side(k):
        return 1 - odd if k == 0 else odd

    def tie_row(k):
        return tie_index[pl.ds(side(k), 1), :]

    def build_pick(k):
        wanted = jnp.broadcast_to(tie_row(k), (LANES, slots))
        for b in range(buses // LANES):
            ids = lax.broadcasted_iota(jnp.int32, (LANES, slots), 0) + b * LANES
            pick[b * LANES:(b + 1) * LANES, k * slots:(k + 1) * slots] = one_hot(ids == wanted).astype(jnp.bfloat16)

    small[0].wait()
    build_pick(0)

    def tie_copy(u, k, part):
        span = pl.ds(part * part_rows, part_rows)
        return pltpu.make_async_remote_copy(
            src_ref=snd.at[u, k, span], dst_ref=rcv.at[u, k, span],
            send_sem=send_sem.at[u, k, part], recv_sem=recv_sem.at[u, k, part],
            device_id={"region": (near, far)[k]}, device_id_type=MESH,
        )

    def plan_copy(u, d):
        return pltpu.make_async_remote_copy(
            src_ref=pbuf.at[u, me], dst_ref=pbuf.at[u, me],
            send_sem=psend_sem.at[u, d], recv_sem=precv_sem.at[u, me],
            device_id={"scen": lax.rem(me + d, peers)}, device_id_type=MESH,
        )

    def plan_arrival(u, d):
        src = lax.rem(me + d, peers)
        return pltpu.make_async_remote_copy(
            src_ref=pbuf.at[u, src], dst_ref=pbuf.at[u, src],
            send_sem=psend_sem.at[u, d], recv_sem=precv_sem.at[u, src],
            device_id={"scen": src}, device_id_type=MESH,
        )

    def put_split(value, at, width):
        count = value.shape[0]
        high = value.astype(jnp.bfloat16)
        split[:count, at:at + width] = high
        split[count:2 * count, at:at + width] = (value - high.astype(jnp.float32)).astype(jnp.bfloat16)

    def select(weights, n, count):
        both = jnp.dot(split[:2 * count], weights[:, n * TILE:(n + 1) * TILE], preferred_element_type=jnp.float32)
        return both[:count] + both[count:]

    per_side = slots // TILE

    def split_state(c):
        for n in range(tiles):
            put_split(st[c, :, :, n * TILE:(n + 1) * TILE].reshape(rows, TILE), n * TILE, TILE)

    def gather_ties(u, k):
        for at in range(per_side):
            snd[u, k, :, at * TILE:(at + 1) * TILE] = select(pick, k * per_side + at, rows)

    def send_ties(u, sides):
        for part in range(PARTS):
            for k in sides:
                tie_copy(u, k, part).start()

    def send_plan(u):
        for d in range(1, peers):
            plan_copy(u, d).start()

    def enter():
        pl.semaphore_wait(barrier, 3 + lax.div(place_z + last_z, last_z + 1) + lax.div(2 * last_z - place_z, last_z + 1))

    def greet_far():
        @pl.when(place_z == last_z)
        def _():
            pl.semaphore_signal(token.at[1], inc=1, device_id=lower, device_id_type=MESH)

        @pl.when(place_z > 0)
        def _():
            pl.semaphore_wait(token.at[0], 1)

        @pl.when(place_z < last_z)
        def _():
            pl.semaphore_signal(token.at[0], inc=1, device_id=higher, device_id_type=MESH)
            pl.semaphore_wait(token.at[1], 1)

        @pl.when((place_z > 0) & (place_z < last_z))
        def _():
            pl.semaphore_signal(token.at[1], inc=1, device_id=lower, device_id_type=MESH)

    def start_first():
        for part in range(PARTS):
            load_first(part).wait()
            some = slice(part * part_scens, (part + 1) * part_scens)
            base = part * 2 * part_rows
            for n in range(tiles):
                cols = slice(n * TILE, (n + 1) * TILE)
                value = st[0, some, :, cols].reshape(part_rows, TILE)
                high = value.astype(jnp.bfloat16)
                split[base:base + part_rows, cols] = high
                split[base + part_rows:base + 2 * part_rows, cols] = (value - high.astype(jnp.float32)).astype(jnp.bfloat16)
            gather_first(0, part)
            if part == 0:
                enter()
                if square:
                    pl.semaphore_signal(token.at[2], inc=1, device_id={"region": near}, device_id_type=MESH)
            tie_copy(0, 0, part).start()
        build_pick(1)
        for part in range(PARTS):
            gather_first(1, part)
            if part == 0 and square:
                pl.semaphore_wait(token.at[2], 1)
            tie_copy(0, 1, part).start()
        pbuf[0, me] = jnp.sum(st[0], axis=0)

    def gather_first(k, part):
        base = part * 2 * part_rows
        for at in range(per_side):
            n = k * per_side + at
            both = jnp.dot(split[base:base + 2 * part_rows], pick[:, n * TILE:(n + 1) * TILE], preferred_element_type=jnp.float32)
            snd[0, k, part * part_rows:(part + 1) * part_rows, at * TILE:(at + 1) * TILE] = both[:part_rows] + both[part_rows:]

    def start_chunk(c):
        load(0, s0_hbm, st, c).wait()
        split_state(c)
        for k in range(2):
            gather_ties(c, k)
            send_ties(c, (k,))
        pbuf[c, me] = jnp.sum(st[c], axis=0)

    start_first()
    pl.loop(1, chunks)(start_chunk)

    for copy in small[1:]:
        copy.wait()
    for k in range(2):
        column = jnp.transpose(jnp.broadcast_to(tie_row(k).astype(jnp.float32), (LANES, slots))).astype(jnp.int32)
        limit = jnp.where(side(k) == 0, tie_len[0:1, 0:1], tie_len[0:1, 1:2])
        alive = lax.broadcasted_iota(jnp.int32, (slots, LANES), 0) < limit
        for b in range(buses // LANES):
            ids = lax.broadcasted_iota(jnp.int32, (slots, LANES), 1) + b * LANES
            hot = one_hot((ids == column) & alive)
            place[k * slots:(k + 1) * slots, b * LANES:(b + 1) * LANES] = hot.astype(jnp.bfloat16)
            part = jnp.broadcast_to(jnp.sum(hot, axis=0, keepdims=True), (SUB, LANES))
            if k == 0:
                mrow[:, b * LANES:(b + 1) * LANES] = part
            else:
                mrow[:, b * LANES:(b + 1) * LANES] += part
    arow[...] = 1.0 - step_rate * (tie_weight * mrow[...] + day_weight)
    gens = gen_bus.shape[1]
    column = jnp.transpose(jnp.broadcast_to(gen_bus[...].astype(jnp.float32), (LANES, gens))).astype(jnp.int32)
    caps = jnp.transpose(jnp.broadcast_to(gen_cap[...], (LANES, gens)))
    for b in range(buses // LANES):
        ids = lax.broadcasted_iota(jnp.int32, (gens, LANES), 1) + b * LANES
        part = jnp.sum(jnp.where(ids == column, caps, 0.0), axis=0, keepdims=True)
        urow[:, b * LANES:(b + 1) * LANES] = jnp.broadcast_to(part, (SUB, LANES))
    greet_far()
    pl.loop(0, chunks)(send_plan)
    mat_copy.wait()

    def prepare(sweep, u, c):
        for d in range(1, peers):
            plan_arrival(u, d).wait_recv()
        plan = pbuf[u, 0]
        for src in range(1, peers):
            plan = plan + pbuf[u, src]
        plan = plan / total_scen
        if sweep == SWEEPS - 1:
            plan_out[c] = plan
        for n in range(tiles):
            cols = slice(n * TILE, (n + 1) * TILE)
            now = st[c, :, :, cols]
            day = plan[:, cols]
            base = pr[c, :, :, cols]
            if sweep == 0:
                dual = now - day
                dd[c, :, :, cols] = dual
                pr[c, :, :, cols] = base + (0.5 * tie_weight) * mrow[:, cols] * now
            else:
                dual = dd[c, :, :, cols] + now - day
            kk[:, :, cols] = step_rate * (base + day_weight * (dual - day))
            rb[0, :, cols] = now.reshape(rows, TILE).astype(jnp.bfloat16)
        for n in range(tiles):
            cols = slice(n * TILE, (n + 1) * TILE)
            slope = jnp.dot(rb[0], mat[:, cols], preferred_element_type=jnp.float32).reshape(scens, SUB, TILE)
            first[:, :, cols] = arow[:, cols] * st[c, :, :, cols] - step_rate * slope - kk[:, :, cols]

    def descend(sweep, u, c, parts):
        count = part_rows * len(parts)
        lines = slice(parts[0] * part_rows, parts[0] * part_rows + count)
        some = slice(lines.start // SUB, lines.stop // SUB)
        for k in range(2):
            for part in parts:
                tie_copy(u, k, part).wait_recv()
            put_split(rcv[u, k, lines], k * slots, slots)

        def advance(n, new, step):
            cols = slice(n * TILE, (n + 1) * TILE)
            new = jnp.minimum(jnp.maximum(new, -dm[c, some, :, cols]), urow[:, cols])
            if step < STEPS - 1:
                rb[(step + 1) % 2, lines, cols] = new.reshape(count, TILE).astype(jnp.bfloat16)
            if sweep == SWEEPS - 1 and step == STEPS - 1:
                out[some, pl.ds(pl.multiple_of(c * SUB, SUB), SUB), cols] = new
            else:
                st[c, some, :, cols] = new

        for n in range(tiles):
            cols = slice(n * TILE, (n + 1) * TILE)
            theirs = select(place, n, count).reshape(count // SUB, SUB, TILE)
            if sweep == 0:
                pr[c, some, :, cols] -= (0.5 * tie_weight) * theirs
            pull = (step_rate * tie_weight) * theirs
            kk[some, :, cols] -= pull
            advance(n, first[some, :, cols] + pull, 0)
        for step in range(1, STEPS):
            for n in range(tiles):
                cols = slice(n * TILE, (n + 1) * TILE)
                slope = jnp.dot(rb[step % 2, lines], mat[:, cols], preferred_element_type=jnp.float32).reshape(count // SUB, SUB, TILE)
                advance(n, arow[:, cols] * st[c, some, :, cols] - step_rate * slope - kk[some, :, cols], step)

    every = tuple(range(PARTS))

    @pl.loop(0, chunks)
    def first_sweep(c):
        load(1, price_hbm, pr, c).wait()
        load(2, demand_hbm, dm, c).wait()
        prepare(0, c, c)
        descend(0, c, c, every)
        u = chunks + c
        pbuf[u, me] = jnp.sum(st[c] + dd[c], axis=0)
        send_plan(u)
        split_state(c)
        for k in range(2):
            gather_ties(u, k)
        send_ties(u, (0, 1))

    @pl.loop(0, chunks - 1)
    def last_sweep(c):
        prepare(1, chunks + c, c)
        descend(1, chunks + c, c, every)

    prepare(1, 2 * chunks - 1, chunks - 1)
    for part in every:
        descend(1, 2 * chunks - 1, chunks - 1, (part,))

    def finish(u, carry):
        for k in range(2):
            for part in every:
                tie_copy(u, k, part).wait_send()
        for d in range(1, peers):
            plan_copy(u, d).wait_send()
        return carry

    lax.fori_loop(0, SWEEPS * chunks, finish, 0)


def store(final, plan, final_hbm, plan_hbm, sem):
    copies = (
        pltpu.make_async_copy(final, final_hbm, sem.at[0]),
        pltpu.make_async_copy(plan, plan_hbm, sem.at[1]),
    )
    for copy in copies:
        copy.start()
    for copy in copies:
        copy.wait()


def body(start_state, price, demand, sens, gen_bus, gen_cap, tie_index, tie_len):
    _, scens, hours, buses = start_state.shape
    slots = tie_index.shape[2]
    peers = lax.axis_size("scen")
    regions = lax.axis_size("region")
    chunks = hours // SUB
    rows = scens * SUB
    f32, bf16 = jnp.float32, jnp.bfloat16
    resident = pl.BlockSpec(memory_space=pltpu.VMEM)
    anywhere = pl.BlockSpec(memory_space=pl.ANY)
    whole = pltpu.VMEM((chunks, scens, SUB, buses), f32)
    final, plan = pl.pallas_call(
        functools.partial(kernel, scens * peers, regions, peers),
        out_shape=(
            pltpu.VMEM((scens, hours, buses), f32),
            pltpu.VMEM((chunks, SUB, buses), f32),
        ),
        in_specs=[anywhere] * 8,
        out_specs=(resident, resident),
        scratch_shapes=[
            pltpu.VMEM(gen_bus.shape, gen_bus.dtype),
            pltpu.VMEM(gen_cap.shape, gen_cap.dtype),
            pltpu.VMEM(tie_index.shape[1:], tie_index.dtype),
            pltpu.VMEM(tie_len.shape, tie_len.dtype),
            whole, whole, whole, whole,
            pltpu.VMEM((buses, buses), bf16),
            pltpu.VMEM((buses, 2 * slots), bf16),
            pltpu.VMEM((2 * slots, buses), bf16),
            pltpu.VMEM((SUB, buses), f32),
            pltpu.VMEM((SUB, buses), f32),
            pltpu.VMEM((SUB, buses), f32),
            pltpu.VMEM((2 * rows, buses), bf16),
            pltpu.VMEM((2, rows, buses), bf16),
            pltpu.VMEM((scens, SUB, buses), f32),
            pltpu.VMEM((scens, SUB, buses), f32),
            pltpu.VMEM((SWEEPS * chunks, 2, rows, slots), f32),
            pltpu.VMEM((SWEEPS * chunks, 2, rows, slots), f32),
            pltpu.VMEM((SWEEPS * chunks, peers, SUB, buses), f32),
            pltpu.SemaphoreType.REGULAR((3,)),
            pltpu.SemaphoreType.DMA((4,)),
            pltpu.SemaphoreType.DMA((3, chunks - 1 + PARTS)),
            pltpu.SemaphoreType.DMA,
            pltpu.SemaphoreType.DMA((SWEEPS * chunks, 2, PARTS)),
            pltpu.SemaphoreType.DMA((SWEEPS * chunks, 2, PARTS)),
            pltpu.SemaphoreType.DMA((SWEEPS * chunks, peers)),
            pltpu.SemaphoreType.DMA((SWEEPS * chunks, peers)),
        ],
        compiler_params=pltpu.CompilerParams(collective_id=0, has_side_effects=True),
        name="dispatch",
    )(start_state[0], price[0], demand[0], sens[0], gen_bus, gen_cap, tie_index[0], tie_len)
    final, plan = pl.pallas_call(
        store,
        out_shape=(
            jax.ShapeDtypeStruct(final.shape, f32),
            jax.ShapeDtypeStruct(plan.shape, f32),
        ),
        in_specs=[anywhere] * 2,
        out_specs=(anywhere, anywhere),
        scratch_shapes=[pltpu.SemaphoreType.DMA((2,))],
        name="store",
    )(
        pltpu.with_memory_space_constraint(final, pltpu.VMEM),
        pltpu.with_memory_space_constraint(plan, pltpu.VMEM),
    )
    return (final[None], plan.reshape(1, hours, buses))


def solution(mesh):
    in_specs = (
        P("region", "scen", None, None),
        P("region", "scen", None, None),
        P("region", "scen", None, None),
        P("region", None, None),
        P("region", None),
        P("region", None),
        P("region", None, None),
        P("region", None),
    )
    out_specs = (P("region", "scen", None, None), P("region", None, None))
    return jax.shard_map(body, mesh=mesh, in_specs=in_specs, out_specs=out_specs, check_vma=False)
```

```python
import functools
import jax
import jax.numpy as jnp
from jax import lax
from jax.experimental import pallas as pl
from jax.experimental.pallas import tpu as pltpu
from jax.sharding import PartitionSpec as P

SWEEPS = 2
STEPS = 3
SUB = 8
LANES = 128
TILE = 256
PARTS = 2


step_rate = 0.3
tie_weight = 1.0
day_weight = 0.5

MESH = pl.DeviceIdType.MESH


def kernel(
    total_scen, regions, peers,
    s0_hbm, price_hbm, demand_hbm, sens_hbm, gen_bus_hbm, gen_cap_hbm, tie_index_hbm, tie_len_hbm,
    out, plan_out,
    gen_bus, gen_cap, tie_index, tie_len,
    st, dd, pr, dm, mat, pick, place, mrow, arow, urow, split, rb, kk, first,
    snd, rcv, pbuf,
    token, small_sem, in_sem, mat_sem, send_sem, recv_sem, psend_sem, precv_sem,
):
    chunks, scens, _, buses = st.shape
    slots = tie_index.shape[1]
    rows = scens * SUB
    tiles = buses // TILE
    me = lax.axis_index("scen")
    reg = lax.axis_index("region")
    odd = lax.rem(reg, 2)
    near = reg + 1 - 2 * odd
    far = lax.rem(reg + regions - 1 + 2 * odd, regions)
    square = regions == 4
    across = lax.rem(reg + 2, regions)
    part_rows = rows // PARTS
    part_scens = scens // PARTS
    whole = (0, rows)
    parts = tuple((part * part_rows, part_rows) for part in range(PARTS))
    last = SWEEPS * chunks - 1

    barrier = pltpu.get_barrier_semaphore()
    for other in (near, across if square else far):
        pl.semaphore_signal(barrier, inc=1, device_id={"region": other}, device_id_type=MESH)
    half = lax.rem(me, 2)
    place_z = lax.div(me, 2)
    last_z = peers // 2 - 1
    lower, higher = {"scen": me - 2}, {"scen": me + 2}
    pl.semaphore_signal(barrier, inc=1, device_id={"scen": me + 1 - 2 * half}, device_id_type=MESH)

    @pl.when(place_z > 0)
    def _():
        pl.semaphore_signal(barrier, inc=1, device_id=lower, device_id_type=MESH)

    @pl.when(place_z < last_z)
    def _():
        pl.semaphore_signal(barrier, inc=1, device_id=higher, device_id_type=MESH)

    def load(kind, source, target, c):
        return pltpu.make_async_copy(source.at[:, pl.ds(pl.multiple_of(c * SUB, SUB), SUB), :], target.at[c], in_sem.at[kind, c])

    def load_first(part):
        some = pl.ds(part * part_scens, part_scens)
        return pltpu.make_async_copy(s0_hbm.at[some, pl.ds(0, SUB), :], st.at[0, some], in_sem.at[0, 0 if part == 0 else chunks - 1 + part])

    small = [
        pltpu.make_async_copy(source, target, small_sem.at[i])
        for i, (source, target) in enumerate((
            (tie_index_hbm, tie_index), (tie_len_hbm, tie_len), (gen_bus_hbm, gen_bus), (gen_cap_hbm, gen_cap),
        ))
    ]
    small[0].start()
    for part in range(PARTS):
        load_first(part).start()
    for c in range(1, chunks):
        load(0, s0_hbm, st, c).start()
    for copy in small[1:]:
        copy.start()

    mat_copy = pltpu.make_async_copy(sens_hbm, mat, mat_sem)

    def one_hot(hit):
        return jnp.where(hit, 1.0, 0.0)

    def side(k):
        return 1 - odd if k == 0 else odd

    def tie_row(k):
        return tie_index[pl.ds(side(k), 1), :]

    def build_pick(k, at):
        lanes = slice(at * TILE, (at + 1) * TILE)
        wanted = jnp.broadcast_to(tie_row(k)[:, lanes], (LANES, TILE))
        for b in range(buses // LANES):
            ids = lax.broadcasted_iota(jnp.int32, (LANES, TILE), 0) + b * LANES
            pick[b * LANES:(b + 1) * LANES, k * slots + at * TILE:k * slots + (at + 1) * TILE] = one_hot(ids == wanted).astype(jnp.bfloat16)

    small[0].wait()
    build_pick(0, 0)

    def tie_copy(u, k, span, lanes=slice(None)):
        part = span[0] // part_rows
        block = pl.ds(*span)
        return pltpu.make_async_remote_copy(
            src_ref=snd.at[u, k, block, lanes], dst_ref=rcv.at[u, k, block, lanes],
            send_sem=send_sem.at[u, k, part], recv_sem=recv_sem.at[u, k, part],
            device_id={"region": (near, far)[k]}, device_id_type=MESH,
        )

    def plan_copy(u, d):
        return pltpu.make_async_remote_copy(
            src_ref=pbuf.at[u, me], dst_ref=pbuf.at[u, me],
            send_sem=psend_sem.at[u, d], recv_sem=precv_sem.at[u, me],
            device_id={"scen": lax.rem(me + d, peers)}, device_id_type=MESH,
        )

    def plan_arrival(u, d):
        src = lax.rem(me + d, peers)
        return pltpu.make_async_remote_copy(
            src_ref=pbuf.at[u, src], dst_ref=pbuf.at[u, src],
            send_sem=psend_sem.at[u, d], recv_sem=precv_sem.at[u, src],
            device_id={"scen": src}, device_id_type=MESH,
        )

    def put_split(value, at, width):
        count = value.shape[0]
        high = value.astype(jnp.bfloat16)
        split[:count, at:at + width] = high
        split[count:2 * count, at:at + width] = (value - high.astype(jnp.float32)).astype(jnp.bfloat16)

    def select(weights, n, count):
        both = jnp.dot(split[:2 * count], weights[:, n * TILE:(n + 1) * TILE], preferred_element_type=jnp.float32)
        return both[:count] + both[count:]

    per_side = slots // TILE

    def split_state(c):
        for n in range(tiles):
            put_split(st[c, :, :, n * TILE:(n + 1) * TILE].reshape(rows, TILE), n * TILE, TILE)

    def gather_ties(u, k):
        for at in range(per_side):
            snd[u, k, :, at * TILE:(at + 1) * TILE] = select(pick, k * per_side + at, rows)

    def send_ties(u, spans):
        for span in spans:
            for k in range(2):
                tie_copy(u, k, span).start()

    def send_plan(u):
        for d in range(1, peers):
            plan_copy(u, d).start()

    def enter():
        pl.semaphore_wait(barrier, 3 + lax.div(place_z + last_z, last_z + 1) + lax.div(2 * last_z - place_z, last_z + 1))

    def greet_far():
        @pl.when(place_z == last_z)
        def _():
            pl.semaphore_signal(token.at[1], inc=1, device_id=lower, device_id_type=MESH)

        @pl.when(place_z > 0)
        def _():
            pl.semaphore_wait(token.at[0], 1)

        @pl.when(place_z < last_z)
        def _():
            pl.semaphore_signal(token.at[0], inc=1, device_id=higher, device_id_type=MESH)
            pl.semaphore_wait(token.at[1], 1)

        @pl.when((place_z > 0) & (place_z < last_z))
        def _():
            pl.semaphore_signal(token.at[1], inc=1, device_id=lower, device_id_type=MESH)

    def start_first():
        for part in range(PARTS):
            load_first(part).wait()
            some = slice(part * part_scens, (part + 1) * part_scens)
            base = part * 2 * part_rows
            for n in range(tiles):
                cols = slice(n * TILE, (n + 1) * TILE)
                value = st[0, some, :, cols].reshape(part_rows, TILE)
                high = value.astype(jnp.bfloat16)
                split[base:base + part_rows, cols] = high
                split[base + part_rows:base + 2 * part_rows, cols] = (value - high.astype(jnp.float32)).astype(jnp.bfloat16)
            for at in range(per_side):
                if part == 0 and at > 0:
                    build_pick(0, at)
                gather_first(0, part, at)
                if part == 0 and at == 0:
                    enter()
                    if square:
                        pl.semaphore_signal(token.at[2], inc=1, device_id={"region": near}, device_id_type=MESH)
                first_copy(part, at).start()
        for at in range(per_side):
            build_pick(1, at)
            for part in range(PARTS):
                gather_first(1, part, at)
        if square:
            pl.semaphore_wait(token.at[2], 1)
        tie_copy(0, 1, whole).start()
        mat_copy.start()
        for c in range(chunks):
            load(1, price_hbm, pr, c).start()
            load(2, demand_hbm, dm, c).start()
        pbuf[0, me] = jnp.sum(st[0], axis=0)

    def first_copy(part, at):
        block = pl.ds(part * part_rows, part_rows)
        lanes = pl.ds(at * TILE, TILE)
        return pltpu.make_async_remote_copy(
            src_ref=snd.at[0, 0, block, lanes], dst_ref=rcv.at[0, 0, block, lanes],
            send_sem=send_sem.at[0, 0, 0], recv_sem=recv_sem.at[0, 0, 0],
            device_id={"region": near}, device_id_type=MESH,
        )

    def gather_first(k, part, at):
        base = part * 2 * part_rows
        n = k * per_side + at
        both = jnp.dot(split[base:base + 2 * part_rows], pick[:, n * TILE:(n + 1) * TILE], preferred_element_type=jnp.float32)
        snd[0, k, part * part_rows:(part + 1) * part_rows, at * TILE:(at + 1) * TILE] = both[:part_rows] + both[part_rows:]

    def start_chunk(c):
        load(0, s0_hbm, st, c).wait()
        split_state(c)
        for k in range(2):
            gather_ties(c, k)
            tie_copy(c, k, whole).start()
        pbuf[c, me] = jnp.sum(st[c], axis=0)

    start_first()
    pl.loop(1, chunks)(start_chunk)

    for copy in small[1:]:
        copy.wait()
    for k in range(2):
        column = jnp.transpose(jnp.broadcast_to(tie_row(k).astype(jnp.float32), (LANES, slots))).astype(jnp.int32)
        limit = jnp.where(side(k) == 0, tie_len[0:1, 0:1], tie_len[0:1, 1:2])
        alive = lax.broadcasted_iota(jnp.int32, (slots, LANES), 0) < limit
        for b in range(buses // LANES):
            ids = lax.broadcasted_iota(jnp.int32, (slots, LANES), 1) + b * LANES
            hot = one_hot((ids == column) & alive)
            place[k * slots:(k + 1) * slots, b * LANES:(b + 1) * LANES] = hot.astype(jnp.bfloat16)
            part = jnp.broadcast_to(jnp.sum(hot, axis=0, keepdims=True), (SUB, LANES))
            if k == 0:
                mrow[:, b * LANES:(b + 1) * LANES] = part
            else:
                mrow[:, b * LANES:(b + 1) * LANES] += part
    arow[...] = 1.0 - step_rate * (tie_weight * mrow[...] + day_weight)
    gens = gen_bus.shape[1]
    column = jnp.transpose(jnp.broadcast_to(gen_bus[...].astype(jnp.float32), (LANES, gens))).astype(jnp.int32)
    caps = jnp.transpose(jnp.broadcast_to(gen_cap[...], (LANES, gens)))
    for b in range(buses // LANES):
        ids = lax.broadcasted_iota(jnp.int32, (gens, LANES), 1) + b * LANES
        part = jnp.sum(jnp.where(ids == column, caps, 0.0), axis=0, keepdims=True)
        urow[:, b * LANES:(b + 1) * LANES] = jnp.broadcast_to(part, (SUB, LANES))
    greet_far()
    pl.loop(0, chunks)(send_plan)
    mat_copy.wait()

    def prepare(sweep, u, c):
        for d in range(1, peers):
            plan_arrival(u, d).wait_recv()
        plan = pbuf[u, 0]
        for src in range(1, peers):
            plan = plan + pbuf[u, src]
        plan = plan / total_scen
        if sweep == SWEEPS - 1:
            plan_out[c] = plan
        for n in range(tiles):
            cols = slice(n * TILE, (n + 1) * TILE)
            now = st[c, :, :, cols]
            day = plan[:, cols]
            base = pr[c, :, :, cols]
            if sweep == 0:
                dual = now - day
                dd[c, :, :, cols] = dual
                pr[c, :, :, cols] = base + (0.5 * tie_weight) * mrow[:, cols] * now
            else:
                dual = dd[c, :, :, cols] + now - day
            kk[:, :, cols] = step_rate * (base + day_weight * (dual - day))
            rb[0, :, cols] = now.reshape(rows, TILE).astype(jnp.bfloat16)
        for n in range(tiles):
            cols = slice(n * TILE, (n + 1) * TILE)
            slope = jnp.dot(rb[0], mat[:, cols], preferred_element_type=jnp.float32).reshape(scens, SUB, TILE)
            first[:, :, cols] = arow[:, cols] * st[c, :, :, cols] - step_rate * slope - kk[:, :, cols]

    def descend(sweep, u, c, arrivals):
        top = arrivals[0][0]
        count = sum(span[1] for span in arrivals)
        lines = slice(top, top + count)
        some = slice(lines.start // SUB, lines.stop // SUB)
        for k in range(2):
            for span in arrivals:
                tie_copy(u, k, span).wait_recv()
            put_split(rcv[u, k, lines], k * slots, slots)

        def advance(n, new, step):
            cols = slice(n * TILE, (n + 1) * TILE)
            new = jnp.minimum(jnp.maximum(new, -dm[c, some, :, cols]), urow[:, cols])
            if step < STEPS - 1:
                rb[(step + 1) % 2, lines, cols] = new.reshape(count, TILE).astype(jnp.bfloat16)
            if sweep == SWEEPS - 1 and step == STEPS - 1:
                out[some, pl.ds(pl.multiple_of(c * SUB, SUB), SUB), cols] = new
            else:
                st[c, some, :, cols] = new

        for n in range(tiles):
            cols = slice(n * TILE, (n + 1) * TILE)
            theirs = select(place, n, count).reshape(count // SUB, SUB, TILE)
            if sweep == 0:
                pr[c, some, :, cols] -= (0.5 * tie_weight) * theirs
            pull = (step_rate * tie_weight) * theirs
            kk[some, :, cols] -= pull
            advance(n, first[some, :, cols] + pull, 0)
        for step in range(1, STEPS):
            for n in range(tiles):
                cols = slice(n * TILE, (n + 1) * TILE)
                slope = jnp.dot(rb[step % 2, lines], mat[:, cols], preferred_element_type=jnp.float32).reshape(count // SUB, SUB, TILE)
                advance(n, arow[:, cols] * st[c, some, :, cols] - step_rate * slope - kk[some, :, cols], step)

    @pl.loop(0, chunks)
    def first_sweep(c):
        load(1, price_hbm, pr, c).wait()
        load(2, demand_hbm, dm, c).wait()
        prepare(0, c, c)
        descend(0, c, c, (whole,))
        u = chunks + c
        pbuf[u, me] = jnp.sum(st[c] + dd[c], axis=0)
        send_plan(u)
        split_state(c)
        for k in range(2):
            gather_ties(u, k)

        @pl.when(c < chunks - 1)
        def _():
            send_ties(u, (whole,))

        @pl.when(c == chunks - 1)
        def _():
            send_ties(u, parts)

    @pl.loop(0, chunks - 1)
    def last_sweep(c):
        prepare(1, chunks + c, c)
        descend(1, chunks + c, c, (whole,))

    prepare(1, last, chunks - 1)
    for span in parts:
        descend(1, last, chunks - 1, (span,))

    def finish(u):
        for d in range(1, peers):
            plan_copy(u, d).wait_send()

    pl.loop(0, SWEEPS * chunks)(finish)
    for k in range(2):
        pl.loop(0, last)(lambda u: tie_copy(u, k, whole).wait_send())
        for span in parts:
            tie_copy(last, k, span).wait_send()


def store(final, plan, final_hbm, plan_hbm, sem):
    copies = (
        pltpu.make_async_copy(final, final_hbm, sem.at[0]),
        pltpu.make_async_copy(plan, plan_hbm, sem.at[1]),
    )
    for copy in copies:
        copy.start()
    for copy in copies:
        copy.wait()


def body(start_state, price, demand, sens, gen_bus, gen_cap, tie_index, tie_len):
    _, scens, hours, buses = start_state.shape
    slots = tie_index.shape[2]
    peers = lax.axis_size("scen")
    regions = lax.axis_size("region")
    chunks = hours // SUB
    rows = scens * SUB
    f32, bf16 = jnp.float32, jnp.bfloat16
    resident = pl.BlockSpec(memory_space=pltpu.VMEM)
    anywhere = pl.BlockSpec(memory_space=pl.ANY)
    whole = pltpu.VMEM((chunks, scens, SUB, buses), f32)
    final, plan = pl.pallas_call(
        functools.partial(kernel, scens * peers, regions, peers),
        out_shape=(
            pltpu.VMEM((scens, hours, buses), f32),
            pltpu.VMEM((chunks, SUB, buses), f32),
        ),
        in_specs=[anywhere] * 8,
        out_specs=(resident, resident),
        scratch_shapes=[
            pltpu.VMEM(gen_bus.shape, gen_bus.dtype),
            pltpu.VMEM(gen_cap.shape, gen_cap.dtype),
            pltpu.VMEM(tie_index.shape[1:], tie_index.dtype),
            pltpu.VMEM(tie_len.shape, tie_len.dtype),
            whole, whole, whole, whole,
            pltpu.VMEM((buses, buses), bf16),
            pltpu.VMEM((buses, 2 * slots), bf16),
            pltpu.VMEM((2 * slots, buses), bf16),
            pltpu.VMEM((SUB, buses), f32),
            pltpu.VMEM((SUB, buses), f32),
            pltpu.VMEM((SUB, buses), f32),
            pltpu.VMEM((2 * rows, buses), bf16),
            pltpu.VMEM((2, rows, buses), bf16),
            pltpu.VMEM((scens, SUB, buses), f32),
            pltpu.VMEM((scens, SUB, buses), f32),
            pltpu.VMEM((SWEEPS * chunks, 2, rows, slots), f32),
            pltpu.VMEM((SWEEPS * chunks, 2, rows, slots), f32),
            pltpu.VMEM((SWEEPS * chunks, peers, SUB, buses), f32),
            pltpu.SemaphoreType.REGULAR((3,)),
            pltpu.SemaphoreType.DMA((4,)),
            pltpu.SemaphoreType.DMA((3, chunks - 1 + PARTS)),
            pltpu.SemaphoreType.DMA,
            pltpu.SemaphoreType.DMA((SWEEPS * chunks, 2, PARTS)),
            pltpu.SemaphoreType.DMA((SWEEPS * chunks, 2, PARTS)),
            pltpu.SemaphoreType.DMA((SWEEPS * chunks, peers)),
            pltpu.SemaphoreType.DMA((SWEEPS * chunks, peers)),
        ],
        compiler_params=pltpu.CompilerParams(collective_id=0, has_side_effects=True),
        name="dispatch",
    )(start_state[0], price[0], demand[0], sens[0], gen_bus, gen_cap, tie_index[0], tie_len)
    final, plan = pl.pallas_call(
        store,
        out_shape=(
            jax.ShapeDtypeStruct(final.shape, f32),
            jax.ShapeDtypeStruct(plan.shape, f32),
        ),
        in_specs=[anywhere] * 2,
        out_specs=(anywhere, anywhere),
        scratch_shapes=[pltpu.SemaphoreType.DMA((2,))],
        name="store",
    )(
        pltpu.with_memory_space_constraint(final, pltpu.VMEM),
        pltpu.with_memory_space_constraint(plan, pltpu.VMEM),
    )
    return (final[None], plan.reshape(1, hours, buses))


def solution(mesh):
    in_specs = (
        P("region", "scen", None, None),
        P("region", "scen", None, None),
        P("region", "scen", None, None),
        P("region", None, None),
        P("region", None),
        P("region", None),
        P("region", None, None),
        P("region", None),
    )
    out_specs = (P("region", "scen", None, None), P("region", None, None))
    return jax.shard_map(body, mesh=mesh, in_specs=in_specs, out_specs=out_specs, check_vma=False)
```

```python
import functools
import jax
import jax.numpy as jnp
from jax import lax
from jax.experimental import pallas as pl
from jax.experimental.pallas import tpu as pltpu
from jax.sharding import PartitionSpec as P

SWEEPS = 2
STEPS = 3
SUB = 8
LANES = 128
TILE = 256
PARTS = 2


step_rate = 0.3
tie_weight = 1.0
day_weight = 0.5

MESH = pl.DeviceIdType.MESH


def kernel(
    total_scen, regions, peers,
    s0_hbm, price_hbm, demand_hbm, sens_hbm, gen_bus_hbm, gen_cap_hbm, tie_index_hbm, tie_len_hbm,
    out, plan_out,
    gen_bus, gen_cap, tie_index, tie_len,
    st, dd, pr, dm, mat, pick, place, mrow, arow, urow, split, rb, kk, first,
    snd, rcv, pbuf,
    token, small_sem, in_sem, mat_sem, send_sem, recv_sem, psend_sem, precv_sem,
):
    chunks, scens, _, buses = st.shape
    slots = tie_index.shape[1]
    rows = scens * SUB
    tiles = buses // TILE
    me = lax.axis_index("scen")
    reg = lax.axis_index("region")
    odd = lax.rem(reg, 2)
    near = reg + 1 - 2 * odd
    far = lax.rem(reg + regions - 1 + 2 * odd, regions)
    square = regions == 4
    across = lax.rem(reg + 2, regions)
    row = lax.div(reg, 2)
    part_rows = rows // PARTS
    part_scens = scens // PARTS
    whole = (0, rows)
    parts = tuple((part * part_rows, part_rows) for part in range(PARTS))
    last = SWEEPS * chunks - 1

    barrier = pltpu.get_barrier_semaphore()
    for other in (near, across if square else far):
        pl.semaphore_signal(barrier, inc=1, device_id={"region": other}, device_id_type=MESH)
    half = lax.rem(me, 2)
    place_z = lax.div(me, 2)
    last_z = peers // 2 - 1
    lower, higher = {"scen": me - 2}, {"scen": me + 2}
    pl.semaphore_signal(barrier, inc=1, device_id={"scen": me + 1 - 2 * half}, device_id_type=MESH)

    @pl.when(place_z > 0)
    def _():
        pl.semaphore_signal(barrier, inc=1, device_id=lower, device_id_type=MESH)

    @pl.when(place_z < last_z)
    def _():
        pl.semaphore_signal(barrier, inc=1, device_id=higher, device_id_type=MESH)

    def load(kind, source, target, c):
        return pltpu.make_async_copy(source.at[:, pl.ds(pl.multiple_of(c * SUB, SUB), SUB), :], target.at[c], in_sem.at[kind, c])

    def load_first(part):
        some = pl.ds(part * part_scens, part_scens)
        return pltpu.make_async_copy(s0_hbm.at[some, pl.ds(0, SUB), :], st.at[0, some], in_sem.at[0, 0 if part == 0 else chunks - 1 + part])

    small = [
        pltpu.make_async_copy(source, target, small_sem.at[i])
        for i, (source, target) in enumerate((
            (tie_index_hbm, tie_index), (tie_len_hbm, tie_len), (gen_bus_hbm, gen_bus), (gen_cap_hbm, gen_cap),
        ))
    ]
    small[0].start()
    for part in range(PARTS):
        load_first(part).start()
    for c in range(1, chunks):
        load(0, s0_hbm, st, c).start()
    for copy in small[1:]:
        copy.start()

    mat_copy = pltpu.make_async_copy(sens_hbm, mat, mat_sem)

    def one_hot(hit):
        return jnp.where(hit, 1.0, 0.0)

    def side(k):
        return 1 - odd if k == 0 else odd

    def tie_row(k):
        return tie_index[pl.ds(side(k), 1), :]

    def build_pick(k, at):
        lanes = slice(at * TILE, (at + 1) * TILE)
        wanted = jnp.broadcast_to(tie_row(k)[:, lanes], (LANES, TILE))
        for b in range(buses // LANES):
            ids = lax.broadcasted_iota(jnp.int32, (LANES, TILE), 0) + b * LANES
            pick[b * LANES:(b + 1) * LANES, k * slots + at * TILE:k * slots + (at + 1) * TILE] = one_hot(ids == wanted).astype(jnp.bfloat16)

    small[0].wait()
    build_pick(0, 0)

    def tie_copy(u, k, span, lanes=slice(None)):
        part = span[0] // part_rows
        block = pl.ds(*span)
        return pltpu.make_async_remote_copy(
            src_ref=snd.at[u, k, block, lanes], dst_ref=rcv.at[u, k, block, lanes],
            send_sem=send_sem.at[u, k, part], recv_sem=recv_sem.at[u, k, part],
            device_id={"region": jnp.where(k == 0, near, far)}, device_id_type=MESH,
        )

    def plan_copy(u, d):
        return pltpu.make_async_remote_copy(
            src_ref=pbuf.at[u, me], dst_ref=pbuf.at[u, me],
            send_sem=psend_sem.at[u, d], recv_sem=precv_sem.at[u, me],
            device_id={"scen": lax.rem(me + d, peers)}, device_id_type=MESH,
        )

    def plan_arrival(u, d):
        src = lax.rem(me + d, peers)
        return pltpu.make_async_remote_copy(
            src_ref=pbuf.at[u, src], dst_ref=pbuf.at[u, src],
            send_sem=psend_sem.at[u, d], recv_sem=precv_sem.at[u, src],
            device_id={"scen": src}, device_id_type=MESH,
        )

    def put_split(value, at, width):
        count = value.shape[0]
        high = value.astype(jnp.bfloat16)
        split[:count, at:at + width] = high
        split[count:2 * count, at:at + width] = (value - high.astype(jnp.float32)).astype(jnp.bfloat16)

    def select(weights, n, count):
        both = jnp.dot(split[:2 * count], weights[:, n * TILE:(n + 1) * TILE], preferred_element_type=jnp.float32)
        return both[:count] + both[count:]

    per_side = slots // TILE

    def split_state(c):
        for n in range(tiles):
            put_split(st[c, :, :, n * TILE:(n + 1) * TILE].reshape(rows, TILE), n * TILE, TILE)

    def gather_ties(u, k):
        for at in range(per_side):
            snd[u, k, :, at * TILE:(at + 1) * TILE] = select(pick, k * per_side + at, rows)

    def send_ties(u, spans, sides=(0, 1)):
        for k in sides:
            for span in spans:
                tie_copy(u, k, span).start()

    def send_plan(u):
        for d in range(1, peers):
            plan_copy(u, d).start()

    def enter():
        pl.semaphore_wait(barrier, 3 + lax.div(place_z + last_z, last_z + 1) + lax.div(2 * last_z - place_z, last_z + 1))

    def greet_far():
        @pl.when(place_z == last_z)
        def _():
            pl.semaphore_signal(token.at[1], inc=1, device_id=lower, device_id_type=MESH)

        @pl.when(place_z > 0)
        def _():
            pl.semaphore_wait(token.at[0], 1)

        @pl.when(place_z < last_z)
        def _():
            pl.semaphore_signal(token.at[0], inc=1, device_id=higher, device_id_type=MESH)
            pl.semaphore_wait(token.at[1], 1)

        @pl.when((place_z > 0) & (place_z < last_z))
        def _():
            pl.semaphore_signal(token.at[1], inc=1, device_id=lower, device_id_type=MESH)

    def start_first():
        for part in range(PARTS):
            load_first(part).wait()
            some = slice(part * part_scens, (part + 1) * part_scens)
            base = part * 2 * part_rows
            for n in range(tiles):
                cols = slice(n * TILE, (n + 1) * TILE)
                value = st[0, some, :, cols].reshape(part_rows, TILE)
                high = value.astype(jnp.bfloat16)
                split[base:base + part_rows, cols] = high
                split[base + part_rows:base + 2 * part_rows, cols] = (value - high.astype(jnp.float32)).astype(jnp.bfloat16)
            for at in range(per_side):
                if part == 0 and at > 0:
                    build_pick(0, at)
                gather_first(0, part, at)
                if part == 0 and at == 0:
                    enter()
                    if square:
                        pl.semaphore_signal(token.at[2], inc=1, device_id={"region": near}, device_id_type=MESH)
                first_copy(part, at).start()
        for at in range(per_side):
            build_pick(1, at)
            for part in range(PARTS):
                gather_first(1, part, at)
        if square:
            pl.semaphore_wait(token.at[2], 1)
        tie_copy(0, 1, whole).start()
        mat_copy.start()
        for c in range(chunks):
            load(1, price_hbm, pr, c).start()
            load(2, demand_hbm, dm, c).start()
        pbuf[0, me] = jnp.sum(st[0], axis=0)

    def first_copy(part, at):
        block = pl.ds(part * part_rows, part_rows)
        lanes = pl.ds(at * TILE, TILE)
        return pltpu.make_async_remote_copy(
            src_ref=snd.at[0, 0, block, lanes], dst_ref=rcv.at[0, 0, block, lanes],
            send_sem=send_sem.at[0, 0, 0], recv_sem=recv_sem.at[0, 0, 0],
            device_id={"region": near}, device_id_type=MESH,
        )

    def gather_first(k, part, at):
        base = part * 2 * part_rows
        n = k * per_side + at
        both = jnp.dot(split[base:base + 2 * part_rows], pick[:, n * TILE:(n + 1) * TILE], preferred_element_type=jnp.float32)
        snd[0, k, part * part_rows:(part + 1) * part_rows, at * TILE:(at + 1) * TILE] = both[:part_rows] + both[part_rows:]

    def start_chunk(c):
        load(0, s0_hbm, st, c).wait()
        split_state(c)
        for k in range(2):
            gather_ties(c, k)
            tie_copy(c, k, whole).start()
        pbuf[c, me] = jnp.sum(st[c], axis=0)

    start_first()
    pl.loop(1, chunks)(start_chunk)

    for copy in small[1:]:
        copy.wait()
    for k in range(2):
        column = jnp.transpose(jnp.broadcast_to(tie_row(k).astype(jnp.float32), (LANES, slots))).astype(jnp.int32)
        limit = jnp.where(side(k) == 0, tie_len[0:1, 0:1], tie_len[0:1, 1:2])
        alive = lax.broadcasted_iota(jnp.int32, (slots, LANES), 0) < limit
        for b in range(buses // LANES):
            ids = lax.broadcasted_iota(jnp.int32, (slots, LANES), 1) + b * LANES
            hot = one_hot((ids == column) & alive)
            place[k * slots:(k + 1) * slots, b * LANES:(b + 1) * LANES] = hot.astype(jnp.bfloat16)
            part = jnp.broadcast_to(jnp.sum(hot, axis=0, keepdims=True), (SUB, LANES))
            if k == 0:
                mrow[:, b * LANES:(b + 1) * LANES] = part
            else:
                mrow[:, b * LANES:(b + 1) * LANES] += part
    arow[...] = 1.0 - step_rate * (tie_weight * mrow[...] + day_weight)
    gens = gen_bus.shape[1]
    column = jnp.transpose(jnp.broadcast_to(gen_bus[...].astype(jnp.float32), (LANES, gens))).astype(jnp.int32)
    caps = jnp.transpose(jnp.broadcast_to(gen_cap[...], (LANES, gens)))
    for b in range(buses // LANES):
        ids = lax.broadcasted_iota(jnp.int32, (gens, LANES), 1) + b * LANES
        part = jnp.sum(jnp.where(ids == column, caps, 0.0), axis=0, keepdims=True)
        urow[:, b * LANES:(b + 1) * LANES] = jnp.broadcast_to(part, (SUB, LANES))
    greet_far()
    pl.loop(0, chunks)(send_plan)
    mat_copy.wait()

    def prepare(sweep, u, c):
        for d in range(1, peers):
            plan_arrival(u, d).wait_recv()
        plan = pbuf[u, 0]
        for src in range(1, peers):
            plan = plan + pbuf[u, src]
        plan = plan / total_scen
        if sweep == SWEEPS - 1:
            plan_out[c] = plan
        for n in range(tiles):
            cols = slice(n * TILE, (n + 1) * TILE)
            now = st[c, :, :, cols]
            day = plan[:, cols]
            base = pr[c, :, :, cols]
            if sweep == 0:
                dual = now - day
                dd[c, :, :, cols] = dual
                pr[c, :, :, cols] = base + (0.5 * tie_weight) * mrow[:, cols] * now
            else:
                dual = dd[c, :, :, cols] + now - day
            kk[:, :, cols] = step_rate * (base + day_weight * (dual - day))
            rb[0, :, cols] = now.reshape(rows, TILE).astype(jnp.bfloat16)
        for n in range(tiles):
            cols = slice(n * TILE, (n + 1) * TILE)
            slope = jnp.dot(rb[0], mat[:, cols], preferred_element_type=jnp.float32).reshape(scens, SUB, TILE)
            first[:, :, cols] = arow[:, cols] * st[c, :, :, cols] - step_rate * slope - kk[:, :, cols]

    def descend(sweep, u, c, arrivals):
        top = arrivals[0][0]
        count = sum(span[1] for span in arrivals)
        lines = slice(top, top + count)
        some = slice(lines.start // SUB, lines.stop // SUB)
        for k in range(2):
            for span in arrivals:
                tie_copy(u, k, span).wait_recv()
            put_split(rcv[u, k, lines], k * slots, slots)

        def advance(n, new, step):
            cols = slice(n * TILE, (n + 1) * TILE)
            new = jnp.minimum(jnp.maximum(new, -dm[c, some, :, cols]), urow[:, cols])
            if step < STEPS - 1:
                rb[(step + 1) % 2, lines, cols] = new.reshape(count, TILE).astype(jnp.bfloat16)
            if sweep == SWEEPS - 1 and step == STEPS - 1:
                out[some, pl.ds(pl.multiple_of(c * SUB, SUB), SUB), cols] = new
            else:
                st[c, some, :, cols] = new

        for n in range(tiles):
            cols = slice(n * TILE, (n + 1) * TILE)
            theirs = select(place, n, count).reshape(count // SUB, SUB, TILE)
            if sweep == 0:
                pr[c, some, :, cols] -= (0.5 * tie_weight) * theirs
            pull = (step_rate * tie_weight) * theirs
            kk[some, :, cols] -= pull
            advance(n, first[some, :, cols] + pull, 0)
        for step in range(1, STEPS):
            for n in range(tiles):
                cols = slice(n * TILE, (n + 1) * TILE)
                slope = jnp.dot(rb[step % 2, lines], mat[:, cols], preferred_element_type=jnp.float32).reshape(count // SUB, SUB, TILE)
                advance(n, arow[:, cols] * st[c, some, :, cols] - step_rate * slope - kk[some, :, cols], step)

    @pl.loop(0, chunks)
    def first_sweep(c):
        load(1, price_hbm, pr, c).wait()
        load(2, demand_hbm, dm, c).wait()
        prepare(0, c, c)
        descend(0, c, c, (whole,))
        u = chunks + c
        pbuf[u, me] = jnp.sum(st[c] + dd[c], axis=0)
        send_plan(u)
        split_state(c)
        for k in range(2):
            gather_ties(u, k)

        @pl.when(c < chunks - 1)
        def _():
            send_ties(u, (whole,))

        @pl.when(c == chunks - 1)
        def _():
            send_ties(u, parts, (row, 1 - row) if square else (0, 1))

    @pl.loop(0, chunks - 1)
    def last_sweep(c):
        prepare(1, chunks + c, c)
        descend(1, chunks + c, c, (whole,))

    prepare(1, last, chunks - 1)
    for span in parts:
        descend(1, last, chunks - 1, (span,))

    def finish(u):
        for d in range(1, peers):
            plan_copy(u, d).wait_send()

    pl.loop(0, SWEEPS * chunks)(finish)
    for k in range(2):
        pl.loop(0, last)(lambda u: tie_copy(u, k, whole).wait_send())
        for span in parts:
            tie_copy(last, k, span).wait_send()


def store(final, plan, final_hbm, plan_hbm, sem):
    copies = (
        pltpu.make_async_copy(final, final_hbm, sem.at[0]),
        pltpu.make_async_copy(plan, plan_hbm, sem.at[1]),
    )
    for copy in copies:
        copy.start()
    for copy in copies:
        copy.wait()


def body(start_state, price, demand, sens, gen_bus, gen_cap, tie_index, tie_len):
    _, scens, hours, buses = start_state.shape
    slots = tie_index.shape[2]
    peers = lax.axis_size("scen")
    regions = lax.axis_size("region")
    chunks = hours // SUB
    rows = scens * SUB
    f32, bf16 = jnp.float32, jnp.bfloat16
    resident = pl.BlockSpec(memory_space=pltpu.VMEM)
    anywhere = pl.BlockSpec(memory_space=pl.ANY)
    whole = pltpu.VMEM((chunks, scens, SUB, buses), f32)
    final, plan = pl.pallas_call(
        functools.partial(kernel, scens * peers, regions, peers),
        out_shape=(
            pltpu.VMEM((scens, hours, buses), f32),
            pltpu.VMEM((chunks, SUB, buses), f32),
        ),
        in_specs=[anywhere] * 8,
        out_specs=(resident, resident),
        scratch_shapes=[
            pltpu.VMEM(gen_bus.shape, gen_bus.dtype),
            pltpu.VMEM(gen_cap.shape, gen_cap.dtype),
            pltpu.VMEM(tie_index.shape[1:], tie_index.dtype),
            pltpu.VMEM(tie_len.shape, tie_len.dtype),
            whole, whole, whole, whole,
            pltpu.VMEM((buses, buses), bf16),
            pltpu.VMEM((buses, 2 * slots), bf16),
            pltpu.VMEM((2 * slots, buses), bf16),
            pltpu.VMEM((SUB, buses), f32),
            pltpu.VMEM((SUB, buses), f32),
            pltpu.VMEM((SUB, buses), f32),
            pltpu.VMEM((2 * rows, buses), bf16),
            pltpu.VMEM((2, rows, buses), bf16),
            pltpu.VMEM((scens, SUB, buses), f32),
            pltpu.VMEM((scens, SUB, buses), f32),
            pltpu.VMEM((SWEEPS * chunks, 2, rows, slots), f32),
            pltpu.VMEM((SWEEPS * chunks, 2, rows, slots), f32),
            pltpu.VMEM((SWEEPS * chunks, peers, SUB, buses), f32),
            pltpu.SemaphoreType.REGULAR((3,)),
            pltpu.SemaphoreType.DMA((4,)),
            pltpu.SemaphoreType.DMA((3, chunks - 1 + PARTS)),
            pltpu.SemaphoreType.DMA,
            pltpu.SemaphoreType.DMA((SWEEPS * chunks, 2, PARTS)),
            pltpu.SemaphoreType.DMA((SWEEPS * chunks, 2, PARTS)),
            pltpu.SemaphoreType.DMA((SWEEPS * chunks, peers)),
            pltpu.SemaphoreType.DMA((SWEEPS * chunks, peers)),
        ],
        compiler_params=pltpu.CompilerParams(collective_id=0, has_side_effects=True),
        name="dispatch",
    )(start_state[0], price[0], demand[0], sens[0], gen_bus, gen_cap, tie_index[0], tie_len)
    final, plan = pl.pallas_call(
        store,
        out_shape=(
            jax.ShapeDtypeStruct(final.shape, f32),
            jax.ShapeDtypeStruct(plan.shape, f32),
        ),
        in_specs=[anywhere] * 2,
        out_specs=(anywhere, anywhere),
        scratch_shapes=[pltpu.SemaphoreType.DMA((2,))],
        name="store",
    )(
        pltpu.with_memory_space_constraint(final, pltpu.VMEM),
        pltpu.with_memory_space_constraint(plan, pltpu.VMEM),
    )
    return (final[None], plan.reshape(1, hours, buses))


def solution(mesh):
    in_specs = (
        P("region", "scen", None, None),
        P("region", "scen", None, None),
        P("region", "scen", None, None),
        P("region", None, None),
        P("region", None),
        P("region", None),
        P("region", None, None),
        P("region", None),
    )
    out_specs = (P("region", "scen", None, None), P("region", None, None))
    return jax.shard_map(body, mesh=mesh, in_specs=in_specs, out_specs=out_specs, check_vma=False)
```

```python
import functools
import jax
import jax.numpy as jnp
from jax import lax
from jax.experimental import pallas as pl
from jax.experimental.pallas import tpu as pltpu
from jax.sharding import PartitionSpec as P

SWEEPS = 2
STEPS = 3
SUB = 8
LANES = 128
TILE = 256
PARTS = 2


step_rate = 0.3
tie_weight = 1.0
day_weight = 0.5

MESH = pl.DeviceIdType.MESH


def kernel(
    total_scen, regions, peers,
    s0_hbm, price_hbm, demand_hbm, sens_hbm, gen_bus_hbm, gen_cap_hbm, tie_index_hbm, tie_len_hbm,
    out, plan_out, dm, mat, place, arow, urow, split, kk, first,
    gen_bus, gen_cap, tie_index, tie_len,
    st, dd, pr, pick, mrow, rb,
    snd, rcv, pbuf,
    token, small_sem, in_sem, mat_sem, send_sem, recv_sem, psend_sem, precv_sem,
):
    chunks, scens, _, buses = st.shape
    slots = tie_index.shape[1]
    rows = scens * SUB
    tiles = buses // TILE
    me = lax.axis_index("scen")
    reg = lax.axis_index("region")
    odd = lax.rem(reg, 2)
    near = reg + 1 - 2 * odd
    far = lax.rem(reg + regions - 1 + 2 * odd, regions)
    square = regions == 4
    across = lax.rem(reg + 2, regions)
    row = lax.div(reg, 2)
    part_rows = rows // PARTS
    part_scens = scens // PARTS
    whole = (0, rows)
    parts = tuple((part * part_rows, part_rows) for part in range(PARTS))
    last = SWEEPS * chunks - 1

    barrier = pltpu.get_barrier_semaphore()
    for other in (near, across if square else far):
        pl.semaphore_signal(barrier, inc=1, device_id={"region": other}, device_id_type=MESH)
    half = lax.rem(me, 2)
    place_z = lax.div(me, 2)
    last_z = peers // 2 - 1
    lower, higher = {"scen": me - 2}, {"scen": me + 2}
    pl.semaphore_signal(barrier, inc=1, device_id={"scen": me + 1 - 2 * half}, device_id_type=MESH)

    @pl.when(place_z > 0)
    def _():
        pl.semaphore_signal(barrier, inc=1, device_id=lower, device_id_type=MESH)

    @pl.when(place_z < last_z)
    def _():
        pl.semaphore_signal(barrier, inc=1, device_id=higher, device_id_type=MESH)

    def load(kind, source, target, c):
        return pltpu.make_async_copy(source.at[:, pl.ds(pl.multiple_of(c * SUB, SUB), SUB), :], target.at[c], in_sem.at[kind, c])

    def load_first(part):
        some = pl.ds(part * part_scens, part_scens)
        return pltpu.make_async_copy(s0_hbm.at[some, pl.ds(0, SUB), :], st.at[0, some], in_sem.at[0, 0 if part == 0 else chunks - 1 + part])

    small = [
        pltpu.make_async_copy(source, target, small_sem.at[i])
        for i, (source, target) in enumerate((
            (tie_index_hbm, tie_index), (tie_len_hbm, tie_len), (gen_bus_hbm, gen_bus), (gen_cap_hbm, gen_cap),
        ))
    ]
    small[0].start()
    for part in range(PARTS):
        load_first(part).start()
    for c in range(1, chunks):
        load(0, s0_hbm, st, c).start()
    for copy in small[1:]:
        copy.start()

    mat_copy = pltpu.make_async_copy(sens_hbm, mat, mat_sem)

    def one_hot(hit):
        return jnp.where(hit, 1.0, 0.0)

    def side(k):
        return 1 - odd if k == 0 else odd

    def tie_row(k):
        return tie_index[pl.ds(side(k), 1), :]

    def build_pick(k, at):
        lanes = slice(at * TILE, (at + 1) * TILE)
        wanted = jnp.broadcast_to(tie_row(k)[:, lanes], (LANES, TILE))
        for b in range(buses // LANES):
            ids = lax.broadcasted_iota(jnp.int32, (LANES, TILE), 0) + b * LANES
            pick[b * LANES:(b + 1) * LANES, k * slots + at * TILE:k * slots + (at + 1) * TILE] = one_hot(ids == wanted).astype(jnp.bfloat16)

    small[0].wait()
    build_pick(0, 0)

    def tie_copy(u, k, span, lanes=slice(None)):
        part = span[0] // part_rows
        block = pl.ds(*span)
        return pltpu.make_async_remote_copy(
            src_ref=snd.at[u, k, block, lanes], dst_ref=rcv.at[u, k, block, lanes],
            send_sem=send_sem.at[u, k, part], recv_sem=recv_sem.at[u, k, part],
            device_id={"region": jnp.where(k == 0, near, far)}, device_id_type=MESH,
        )

    def plan_copy(u, d):
        return pltpu.make_async_remote_copy(
            src_ref=pbuf.at[u, me], dst_ref=pbuf.at[u, me],
            send_sem=psend_sem.at[u, d], recv_sem=precv_sem.at[u, me],
            device_id={"scen": lax.rem(me + d, peers)}, device_id_type=MESH,
        )

    def plan_arrival(u, d):
        src = lax.rem(me + d, peers)
        return pltpu.make_async_remote_copy(
            src_ref=pbuf.at[u, src], dst_ref=pbuf.at[u, src],
            send_sem=psend_sem.at[u, d], recv_sem=precv_sem.at[u, src],
            device_id={"scen": src}, device_id_type=MESH,
        )

    def put_split(value, at, width):
        count = value.shape[0]
        high = value.astype(jnp.bfloat16)
        split[:count, at:at + width] = high
        split[count:2 * count, at:at + width] = (value - high.astype(jnp.float32)).astype(jnp.bfloat16)

    def select(weights, n, count):
        both = jnp.dot(split[:2 * count], weights[:, n * TILE:(n + 1) * TILE], preferred_element_type=jnp.float32)
        return both[:count] + both[count:]

    per_side = slots // TILE

    def split_state(c):
        for n in range(tiles):
            put_split(st[c, :, :, n * TILE:(n + 1) * TILE].reshape(rows, TILE), n * TILE, TILE)

    def gather_ties(u, k):
        for at in range(per_side):
            snd[u, k, :, at * TILE:(at + 1) * TILE] = select(pick, k * per_side + at, rows)

    def send_ties(u, spans, sides=(0, 1)):
        for k in sides:
            for span in spans:
                tie_copy(u, k, span).start()

    def send_plan(u):
        for d in range(1, peers):
            plan_copy(u, d).start()

    def enter():
        pl.semaphore_wait(barrier, 3 + lax.div(place_z + last_z, last_z + 1) + lax.div(2 * last_z - place_z, last_z + 1))

    def greet_far():
        @pl.when(place_z == last_z)
        def _():
            pl.semaphore_signal(token.at[1], inc=1, device_id=lower, device_id_type=MESH)

        @pl.when(place_z > 0)
        def _():
            pl.semaphore_wait(token.at[0], 1)

        @pl.when(place_z < last_z)
        def _():
            pl.semaphore_signal(token.at[0], inc=1, device_id=higher, device_id_type=MESH)
            pl.semaphore_wait(token.at[1], 1)

        @pl.when((place_z > 0) & (place_z < last_z))
        def _():
            pl.semaphore_signal(token.at[1], inc=1, device_id=lower, device_id_type=MESH)

    def start_first():
        for part in range(PARTS):
            load_first(part).wait()
            some = slice(part * part_scens, (part + 1) * part_scens)
            base = part * 2 * part_rows
            for n in range(tiles):
                cols = slice(n * TILE, (n + 1) * TILE)
                value = st[0, some, :, cols].reshape(part_rows, TILE)
                high = value.astype(jnp.bfloat16)
                split[base:base + part_rows, cols] = high
                split[base + part_rows:base + 2 * part_rows, cols] = (value - high.astype(jnp.float32)).astype(jnp.bfloat16)
            for at in range(per_side):
                if part == 0 and at > 0:
                    build_pick(0, at)
                gather_first(0, part, at)
                if part == 0 and at == 0:
                    enter()
                    if square:
                        pl.semaphore_signal(token.at[2], inc=1, device_id={"region": near}, device_id_type=MESH)
                first_copy(part, at).start()
        for at in range(per_side):
            build_pick(1, at)
            for part in range(PARTS):
                gather_first(1, part, at)
        if square:
            pl.semaphore_wait(token.at[2], 1)
        tie_copy(0, 1, whole).start()
        mat_copy.start()
        for c in range(chunks):
            load(1, price_hbm, pr, c).start()
            load(2, demand_hbm, dm, c).start()
        pbuf[0, me] = jnp.sum(st[0], axis=0)

    def first_copy(part, at):
        block = pl.ds(part * part_rows, part_rows)
        lanes = pl.ds(at * TILE, TILE)
        return pltpu.make_async_remote_copy(
            src_ref=snd.at[0, 0, block, lanes], dst_ref=rcv.at[0, 0, block, lanes],
            send_sem=send_sem.at[0, 0, 0], recv_sem=recv_sem.at[0, 0, 0],
            device_id={"region": near}, device_id_type=MESH,
        )

    def gather_first(k, part, at):
        base = part * 2 * part_rows
        n = k * per_side + at
        both = jnp.dot(split[base:base + 2 * part_rows], pick[:, n * TILE:(n + 1) * TILE], preferred_element_type=jnp.float32)
        snd[0, k, part * part_rows:(part + 1) * part_rows, at * TILE:(at + 1) * TILE] = both[:part_rows] + both[part_rows:]

    def start_chunk(c):
        load(0, s0_hbm, st, c).wait()
        split_state(c)
        for k in range(2):
            gather_ties(c, k)
            tie_copy(c, k, whole).start()
        pbuf[c, me] = jnp.sum(st[c], axis=0)

    start_first()
    pl.loop(1, chunks)(start_chunk)

    for copy in small[1:]:
        copy.wait()
    for k in range(2):
        column = jnp.transpose(jnp.broadcast_to(tie_row(k).astype(jnp.float32), (LANES, slots))).astype(jnp.int32)
        limit = jnp.where(side(k) == 0, tie_len[0:1, 0:1], tie_len[0:1, 1:2])
        alive = lax.broadcasted_iota(jnp.int32, (slots, LANES), 0) < limit
        for b in range(buses // LANES):
            ids = lax.broadcasted_iota(jnp.int32, (slots, LANES), 1) + b * LANES
            hot = one_hot((ids == column) & alive)
            place[k * slots:(k + 1) * slots, b * LANES:(b + 1) * LANES] = hot.astype(jnp.bfloat16)
            part = jnp.broadcast_to(jnp.sum(hot, axis=0, keepdims=True), (SUB, LANES))
            if k == 0:
                mrow[:, b * LANES:(b + 1) * LANES] = part
            else:
                mrow[:, b * LANES:(b + 1) * LANES] += part
    arow[...] = 1.0 - step_rate * (tie_weight * mrow[...] + day_weight)
    gens = gen_bus.shape[1]
    column = jnp.transpose(jnp.broadcast_to(gen_bus[...].astype(jnp.float32), (LANES, gens))).astype(jnp.int32)
    caps = jnp.transpose(jnp.broadcast_to(gen_cap[...], (LANES, gens)))
    for b in range(buses // LANES):
        ids = lax.broadcasted_iota(jnp.int32, (gens, LANES), 1) + b * LANES
        part = jnp.sum(jnp.where(ids == column, caps, 0.0), axis=0, keepdims=True)
        urow[:, b * LANES:(b + 1) * LANES] = jnp.broadcast_to(part, (SUB, LANES))
    greet_far()
    pl.loop(0, chunks)(send_plan)
    mat_copy.wait()

    def prepare(sweep, u, c):
        for d in range(1, peers):
            plan_arrival(u, d).wait_recv()
        plan = pbuf[u, 0]
        for src in range(1, peers):
            plan = plan + pbuf[u, src]
        plan = plan / total_scen
        if sweep == SWEEPS - 1:
            plan_out[c] = plan
        for n in range(tiles):
            cols = slice(n * TILE, (n + 1) * TILE)
            now = st[c, :, :, cols]
            day = plan[:, cols]
            base = pr[c, :, :, cols]
            if sweep == 0:
                dual = now - day
                dd[c, :, :, cols] = dual
                pr[c, :, :, cols] = base + (0.5 * tie_weight) * mrow[:, cols] * now
            else:
                dual = dd[c, :, :, cols] + now - day
            kk[:, :, cols] = step_rate * (base + day_weight * (dual - day))
            rb[0, :, cols] = now.reshape(rows, TILE).astype(jnp.bfloat16)
        for n in range(tiles):
            cols = slice(n * TILE, (n + 1) * TILE)
            slope = jnp.dot(rb[0], mat[:, cols], preferred_element_type=jnp.float32).reshape(scens, SUB, TILE)
            first[:, :, cols] = arow[:, cols] * st[c, :, :, cols] - step_rate * slope - kk[:, :, cols]

    def descend(sweep, u, c, arrivals):
        top = arrivals[0][0]
        count = sum(span[1] for span in arrivals)
        lines = slice(top, top + count)
        some = slice(lines.start // SUB, lines.stop // SUB)
        for k in range(2):
            for span in arrivals:
                tie_copy(u, k, span).wait_recv()
            put_split(rcv[u, k, lines], k * slots, slots)

        def advance(n, new, step):
            cols = slice(n * TILE, (n + 1) * TILE)
            new = jnp.minimum(jnp.maximum(new, -dm[c, some, :, cols]), urow[:, cols])
            if step < STEPS - 1:
                rb[(step + 1) % 2, lines, cols] = new.reshape(count, TILE).astype(jnp.bfloat16)
            if sweep == SWEEPS - 1 and step == STEPS - 1:
                out[some, pl.ds(pl.multiple_of(c * SUB, SUB), SUB), cols] = new
            else:
                st[c, some, :, cols] = new

        for n in range(tiles):
            cols = slice(n * TILE, (n + 1) * TILE)
            theirs = select(place, n, count).reshape(count // SUB, SUB, TILE)
            if sweep == 0:
                pr[c, some, :, cols] -= (0.5 * tie_weight) * theirs
            pull = (step_rate * tie_weight) * theirs
            kk[some, :, cols] -= pull
            advance(n, first[some, :, cols] + pull, 0)
        for step in range(1, STEPS):
            for n in range(tiles):
                cols = slice(n * TILE, (n + 1) * TILE)
                slope = jnp.dot(rb[step % 2, lines], mat[:, cols], preferred_element_type=jnp.float32).reshape(count // SUB, SUB, TILE)
                advance(n, arow[:, cols] * st[c, some, :, cols] - step_rate * slope - kk[some, :, cols], step)

    @pl.loop(0, chunks)
    def first_sweep(c):
        load(1, price_hbm, pr, c).wait()
        load(2, demand_hbm, dm, c).wait()
        prepare(0, c, c)
        descend(0, c, c, (whole,))
        u = chunks + c
        pbuf[u, me] = jnp.sum(st[c] + dd[c], axis=0)
        send_plan(u)
        split_state(c)
        for k in range(2):
            gather_ties(u, k)

        @pl.when(c < chunks - 1)
        def _():
            send_ties(u, (whole,))

        @pl.when(c == chunks - 1)
        def _():
            send_ties(u, parts, (row, 1 - row) if square else (0, 1))

    @pl.loop(0, chunks - 1)
    def last_sweep(c):
        prepare(1, chunks + c, c)
        descend(1, chunks + c, c, (whole,))

    prepare(1, last, chunks - 1)
    for span in parts[:-1]:
        descend(1, last, chunks - 1, (span,))
    top, count = parts[-1]
    for k in range(2):
        tie_copy(last, k, parts[-1]).wait_recv()
        put_split(rcv[last, k, top:top + count], k * slots, slots)

    def finish(u):
        for d in range(1, peers):
            plan_copy(u, d).wait_send()

    pl.loop(0, SWEEPS * chunks)(finish)
    for k in range(2):
        pl.loop(0, last)(lambda u: tie_copy(u, k, whole).wait_send())
        for span in parts:
            tie_copy(last, k, span).wait_send()


def close(
    out, plan, dm, mat, place, arow, urow, split, kk, first,
    final_hbm, plan_hbm, st, kl, rb, sem,
):
    scens, hours, buses = out.shape
    tiles = buses // TILE
    some = slice(scens - scens // PARTS, scens)
    late = pl.ds(hours - SUB, SUB)
    count = (some.stop - some.start) * SUB
    early = (
        pltpu.make_async_copy(out.at[pl.ds(0, some.start)], final_hbm.at[pl.ds(0, some.start)], sem.at[0]),
        pltpu.make_async_copy(
            out.at[pl.ds(some.start, scens - some.start), pl.ds(0, hours - SUB)],
            final_hbm.at[pl.ds(some.start, scens - some.start), pl.ds(0, hours - SUB)], sem.at[1],
        ),
        pltpu.make_async_copy(plan, plan_hbm, sem.at[2]),
    )
    for copy in early:
        copy.start()
    last = dm.shape[0] - 1

    def advance(n, new, step):
        cols = slice(n * TILE, (n + 1) * TILE)
        new = jnp.minimum(jnp.maximum(new, -dm[last, some, :, cols]), urow[:, cols])
        if step < STEPS - 1:
            rb[step % 2, :, cols] = new.reshape(count, TILE).astype(jnp.bfloat16)
        st[:, :, cols] = new

    for n in range(tiles):
        cols = slice(n * TILE, (n + 1) * TILE)
        both = jnp.dot(split[:2 * count], place[:, cols], preferred_element_type=jnp.float32)
        pull = (step_rate * tie_weight) * (both[:count] + both[count:]).reshape(count // SUB, SUB, TILE)
        kl[:, :, cols] = kk[some, :, cols] - pull
        advance(n, first[some, :, cols] + pull, 0)
    for step in range(1, STEPS):
        for n in range(tiles):
            cols = slice(n * TILE, (n + 1) * TILE)
            slope = jnp.dot(rb[(step - 1) % 2], mat[:, cols], preferred_element_type=jnp.float32).reshape(count // SUB, SUB, TILE)
            advance(n, arow[:, cols] * st[:, :, cols] - step_rate * slope - kl[:, :, cols], step)
    end = pltpu.make_async_copy(st, final_hbm.at[pl.ds(some.start, scens - some.start), late], sem.at[3])
    end.start()
    for copy in early:
        copy.wait()
    end.wait()


def body(start_state, price, demand, sens, gen_bus, gen_cap, tie_index, tie_len):
    _, scens, hours, buses = start_state.shape
    slots = tie_index.shape[2]
    peers = lax.axis_size("scen")
    regions = lax.axis_size("region")
    chunks = hours // SUB
    rows = scens * SUB
    f32, bf16 = jnp.float32, jnp.bfloat16
    resident = pl.BlockSpec(memory_space=pltpu.VMEM)
    anywhere = pl.BlockSpec(memory_space=pl.ANY)
    whole = pltpu.VMEM((chunks, scens, SUB, buses), f32)
    made = pl.pallas_call(
        functools.partial(kernel, scens * peers, regions, peers),
        out_shape=(
            pltpu.VMEM((scens, hours, buses), f32),
            pltpu.VMEM((chunks, SUB, buses), f32),
            whole,
            pltpu.VMEM((buses, buses), bf16),
            pltpu.VMEM((2 * slots, buses), bf16),
            pltpu.VMEM((SUB, buses), f32),
            pltpu.VMEM((SUB, buses), f32),
            pltpu.VMEM((2 * rows, buses), bf16),
            pltpu.VMEM((scens, SUB, buses), f32),
            pltpu.VMEM((scens, SUB, buses), f32),
        ),
        in_specs=[pl.BlockSpec(memory_space=pltpu.HBM)] * 8,
        out_specs=(resident,) * 10,
        scratch_shapes=[
            pltpu.VMEM(gen_bus.shape, gen_bus.dtype),
            pltpu.VMEM(gen_cap.shape, gen_cap.dtype),
            pltpu.VMEM(tie_index.shape[1:], tie_index.dtype),
            pltpu.VMEM(tie_len.shape, tie_len.dtype),
            whole, whole, whole,
            pltpu.VMEM((buses, 2 * slots), bf16),
            pltpu.VMEM((SUB, buses), f32),
            pltpu.VMEM((2, rows, buses), bf16),
            pltpu.VMEM((SWEEPS * chunks, 2, rows, slots), f32),
            pltpu.VMEM((SWEEPS * chunks, 2, rows, slots), f32),
            pltpu.VMEM((SWEEPS * chunks, peers, SUB, buses), f32),
            pltpu.SemaphoreType.REGULAR((3,)),
            pltpu.SemaphoreType.DMA((4,)),
            pltpu.SemaphoreType.DMA((3, chunks - 1 + PARTS)),
            pltpu.SemaphoreType.DMA,
            pltpu.SemaphoreType.DMA((SWEEPS * chunks, 2, PARTS)),
            pltpu.SemaphoreType.DMA((SWEEPS * chunks, 2, PARTS)),
            pltpu.SemaphoreType.DMA((SWEEPS * chunks, peers)),
            pltpu.SemaphoreType.DMA((SWEEPS * chunks, peers)),
        ],
        compiler_params=pltpu.CompilerParams(collective_id=0, has_side_effects=True, vmem_limit_bytes=32 * 2**20),
        name="dispatch",
    )(*(
        pltpu.with_memory_space_constraint(one, pltpu.HBM)
        for one in (start_state[0], price[0], demand[0], sens[0], gen_bus, gen_cap, tie_index[0], tie_len)
    ))
    final, plan = pl.pallas_call(
        close,
        out_shape=(
            jax.ShapeDtypeStruct((scens, hours, buses), f32),
            jax.ShapeDtypeStruct((chunks, SUB, buses), f32),
        ),
        in_specs=[resident] * len(made),
        out_specs=(anywhere, anywhere),
        scratch_shapes=[
            pltpu.VMEM((scens // PARTS, SUB, buses), f32),
            pltpu.VMEM((scens // PARTS, SUB, buses), f32),
            pltpu.VMEM((2, rows // PARTS, buses), bf16),
            pltpu.SemaphoreType.DMA((4,)),
        ],
        compiler_params=pltpu.CompilerParams(vmem_limit_bytes=16 * 2**20),
        name="close",
    )(*(pltpu.with_memory_space_constraint(one, pltpu.VMEM) for one in made))
    return (final[None], plan.reshape(1, hours, buses))


def solution(mesh):
    in_specs = (
        P("region", "scen", None, None),
        P("region", "scen", None, None),
        P("region", "scen", None, None),
        P("region", None, None),
        P("region", None),
        P("region", None),
        P("region", None, None),
        P("region", None),
    )
    out_specs = (P("region", "scen", None, None), P("region", None, None))
    return jax.shard_map(body, mesh=mesh, in_specs=in_specs, out_specs=out_specs, check_vma=False)
```

```python
import functools
import jax
import jax.numpy as jnp
from jax import lax
from jax.experimental import pallas as pl
from jax.experimental.pallas import tpu as pltpu
from jax.sharding import PartitionSpec as P

SWEEPS = 2
STEPS = 3
SUB = 8
LANES = 128
TILE = 256
PARTS = 2


step_rate = 0.3
tie_weight = 1.0
day_weight = 0.5

MESH = pl.DeviceIdType.MESH


def kernel(
    total_scen, regions, peers,
    s0_hbm, price_hbm, demand_hbm, sens_hbm, gen_bus_hbm, gen_cap_hbm, tie_index_hbm, tie_len_hbm,
    out, plan_out, dm, mat, place, arow, urow, split, kk, first,
    gen_bus, gen_cap, tie_index, tie_len,
    st, dd, pr, pick, mrow, rb,
    snd, rcv, pbuf,
    token, small_sem, in_sem, mat_sem, send_sem, recv_sem, psend_sem, precv_sem,
):
    chunks, scens, _, buses = st.shape
    slots = tie_index.shape[1]
    rows = scens * SUB
    tiles = buses // TILE
    me = lax.axis_index("scen")
    reg = lax.axis_index("region")
    odd = lax.rem(reg, 2)
    near = reg + 1 - 2 * odd
    far = lax.rem(reg + regions - 1 + 2 * odd, regions)
    square = regions == 4
    across = lax.rem(reg + 2, regions)
    row = lax.div(reg, 2)
    part_rows = rows // PARTS
    part_scens = scens // PARTS
    whole = (0, rows)
    parts = tuple((part * part_rows, part_rows) for part in range(PARTS))
    last = SWEEPS * chunks - 1

    barrier = pltpu.get_barrier_semaphore()
    for other in (near, across if square else far):
        pl.semaphore_signal(barrier, inc=1, device_id={"region": other}, device_id_type=MESH)
    half = lax.rem(me, 2)
    place_z = lax.div(me, 2)
    last_z = peers // 2 - 1
    lower, higher = {"scen": me - 2}, {"scen": me + 2}
    pl.semaphore_signal(barrier, inc=1, device_id={"scen": me + 1 - 2 * half}, device_id_type=MESH)

    @pl.when(place_z > 0)
    def _():
        pl.semaphore_signal(barrier, inc=1, device_id=lower, device_id_type=MESH)

    @pl.when(place_z < last_z)
    def _():
        pl.semaphore_signal(barrier, inc=1, device_id=higher, device_id_type=MESH)

    def load(kind, source, target, c):
        return pltpu.make_async_copy(source.at[:, pl.ds(pl.multiple_of(c * SUB, SUB), SUB), :], target.at[c], in_sem.at[kind, c])

    def load_first(part):
        some = pl.ds(part * part_scens, part_scens)
        return pltpu.make_async_copy(s0_hbm.at[some, pl.ds(0, SUB), :], st.at[0, some], in_sem.at[0, 0 if part == 0 else chunks - 1 + part])

    small = [
        pltpu.make_async_copy(source, target, small_sem.at[i])
        for i, (source, target) in enumerate((
            (tie_index_hbm, tie_index), (tie_len_hbm, tie_len), (gen_bus_hbm, gen_bus), (gen_cap_hbm, gen_cap),
        ))
    ]
    small[0].start()
    for part in range(PARTS):
        load_first(part).start()
    for c in range(1, chunks):
        load(0, s0_hbm, st, c).start()
    for copy in small[1:]:
        copy.start()

    mat_copy = pltpu.make_async_copy(sens_hbm, mat, mat_sem)

    def one_hot(hit):
        return jnp.where(hit, 1.0, 0.0)

    def side(k):
        return 1 - odd if k == 0 else odd

    def tie_row(k):
        return tie_index[pl.ds(side(k), 1), :]

    def build_pick(k, at):
        lanes = slice(at * TILE, (at + 1) * TILE)
        wanted = jnp.broadcast_to(tie_row(k)[:, lanes], (LANES, TILE))
        for b in range(buses // LANES):
            ids = lax.broadcasted_iota(jnp.int32, (LANES, TILE), 0) + b * LANES
            pick[b * LANES:(b + 1) * LANES, k * slots + at * TILE:k * slots + (at + 1) * TILE] = one_hot(ids == wanted).astype(jnp.bfloat16)

    small[0].wait()
    build_pick(0, 0)

    def tie_copy(u, k, span, lanes=slice(None)):
        part = span[0] // part_rows
        block = pl.ds(*span)
        return pltpu.make_async_remote_copy(
            src_ref=snd.at[u, k, block, lanes], dst_ref=rcv.at[u, k, block, lanes],
            send_sem=send_sem.at[u, k, part], recv_sem=recv_sem.at[u, k, part],
            device_id={"region": jnp.where(k == 0, near, far)}, device_id_type=MESH,
        )

    def plan_copy(u, d):
        return pltpu.make_async_remote_copy(
            src_ref=pbuf.at[u, me], dst_ref=pbuf.at[u, me],
            send_sem=psend_sem.at[u, d], recv_sem=precv_sem.at[u, me],
            device_id={"scen": lax.rem(me + d, peers)}, device_id_type=MESH,
        )

    def plan_arrival(u, d):
        src = lax.rem(me + d, peers)
        return pltpu.make_async_remote_copy(
            src_ref=pbuf.at[u, src], dst_ref=pbuf.at[u, src],
            send_sem=psend_sem.at[u, d], recv_sem=precv_sem.at[u, src],
            device_id={"scen": src}, device_id_type=MESH,
        )

    def put_split(value, at, width):
        count = value.shape[0]
        high = value.astype(jnp.bfloat16)
        split[:count, at:at + width] = high
        split[count:2 * count, at:at + width] = (value - high.astype(jnp.float32)).astype(jnp.bfloat16)

    def select(weights, n, count):
        both = jnp.dot(split[:2 * count], weights[:, n * TILE:(n + 1) * TILE], preferred_element_type=jnp.float32)
        return both[:count] + both[count:]

    per_side = slots // TILE

    def split_state(c):
        for n in range(tiles):
            put_split(st[c, :, :, n * TILE:(n + 1) * TILE].reshape(rows, TILE), n * TILE, TILE)

    def gather_ties(u, k):
        for at in range(per_side):
            snd[u, k, :, at * TILE:(at + 1) * TILE] = select(pick, k * per_side + at, rows)

    def send_ties(u, spans, sides=(0, 1)):
        for k in sides:
            for span in spans:
                tie_copy(u, k, span).start()

    def send_plan(u):
        for d in range(1, peers):
            plan_copy(u, d).start()

    def enter():
        pl.semaphore_wait(barrier, 3 + lax.div(place_z + last_z, last_z + 1) + lax.div(2 * last_z - place_z, last_z + 1))

    def greet_far():
        @pl.when(place_z == last_z)
        def _():
            pl.semaphore_signal(token.at[1], inc=1, device_id=lower, device_id_type=MESH)

        @pl.when(place_z > 0)
        def _():
            pl.semaphore_wait(token.at[0], 1)

        @pl.when(place_z < last_z)
        def _():
            pl.semaphore_signal(token.at[0], inc=1, device_id=higher, device_id_type=MESH)
            pl.semaphore_wait(token.at[1], 1)

        @pl.when((place_z > 0) & (place_z < last_z))
        def _():
            pl.semaphore_signal(token.at[1], inc=1, device_id=lower, device_id_type=MESH)

    def start_first():
        for part in range(PARTS):
            load_first(part).wait()
            some = slice(part * part_scens, (part + 1) * part_scens)
            base = part * 2 * part_rows
            for n in range(tiles):
                cols = slice(n * TILE, (n + 1) * TILE)
                value = st[0, some, :, cols].reshape(part_rows, TILE)
                high = value.astype(jnp.bfloat16)
                split[base:base + part_rows, cols] = high
                split[base + part_rows:base + 2 * part_rows, cols] = (value - high.astype(jnp.float32)).astype(jnp.bfloat16)
            for at in range(per_side):
                if part == 0 and at > 0:
                    build_pick(0, at)
                gather_first(0, part, at)
                if part == 0 and at == 0:
                    enter()
                    if square:
                        pl.semaphore_signal(token.at[2], inc=1, device_id={"region": near}, device_id_type=MESH)
                first_copy(part, at).start()
        for at in range(per_side):
            build_pick(1, at)
            for part in range(PARTS):
                gather_first(1, part, at)
        if square:
            pl.semaphore_wait(token.at[2], 1)
        tie_copy(0, 1, whole).start()
        mat_copy.start()
        for c in range(chunks):
            load(1, price_hbm, pr, c).start()
            load(2, demand_hbm, dm, c).start()
        pbuf[0, me] = jnp.sum(st[0], axis=0)

    def first_copy(part, at):
        block = pl.ds(part * part_rows, part_rows)
        lanes = pl.ds(at * TILE, TILE)
        return pltpu.make_async_remote_copy(
            src_ref=snd.at[0, 0, block, lanes], dst_ref=rcv.at[0, 0, block, lanes],
            send_sem=send_sem.at[0, 0, 0], recv_sem=recv_sem.at[0, 0, 0],
            device_id={"region": near}, device_id_type=MESH,
        )

    def gather_first(k, part, at):
        base = part * 2 * part_rows
        n = k * per_side + at
        both = jnp.dot(split[base:base + 2 * part_rows], pick[:, n * TILE:(n + 1) * TILE], preferred_element_type=jnp.float32)
        snd[0, k, part * part_rows:(part + 1) * part_rows, at * TILE:(at + 1) * TILE] = both[:part_rows] + both[part_rows:]

    def start_chunk(c):
        load(0, s0_hbm, st, c).wait()
        split_state(c)
        for k in range(2):
            gather_ties(c, k)
            tie_copy(c, k, whole).start()
        pbuf[c, me] = jnp.sum(st[c], axis=0)

    start_first()
    pl.loop(1, chunks)(start_chunk)

    for copy in small[1:]:
        copy.wait()
    for k in range(2):
        column = jnp.transpose(jnp.broadcast_to(tie_row(k).astype(jnp.float32), (LANES, slots))).astype(jnp.int32)
        limit = jnp.where(side(k) == 0, tie_len[0:1, 0:1], tie_len[0:1, 1:2])
        alive = lax.broadcasted_iota(jnp.int32, (slots, LANES), 0) < limit
        for b in range(buses // LANES):
            ids = lax.broadcasted_iota(jnp.int32, (slots, LANES), 1) + b * LANES
            hot = one_hot((ids == column) & alive)
            place[k * slots:(k + 1) * slots, b * LANES:(b + 1) * LANES] = hot.astype(jnp.bfloat16)
            part = jnp.broadcast_to(jnp.sum(hot, axis=0, keepdims=True), (SUB, LANES))
            if k == 0:
                mrow[:, b * LANES:(b + 1) * LANES] = part
            else:
                mrow[:, b * LANES:(b + 1) * LANES] += part
    arow[...] = 1.0 - step_rate * (tie_weight * mrow[...] + day_weight)
    gens = gen_bus.shape[1]
    column = jnp.transpose(jnp.broadcast_to(gen_bus[...].astype(jnp.float32), (LANES, gens))).astype(jnp.int32)
    caps = jnp.transpose(jnp.broadcast_to(gen_cap[...], (LANES, gens)))
    for b in range(buses // LANES):
        ids = lax.broadcasted_iota(jnp.int32, (gens, LANES), 1) + b * LANES
        part = jnp.sum(jnp.where(ids == column, caps, 0.0), axis=0, keepdims=True)
        urow[:, b * LANES:(b + 1) * LANES] = jnp.broadcast_to(part, (SUB, LANES))
    greet_far()
    pl.loop(0, chunks)(send_plan)
    mat_copy.wait()

    def prepare(sweep, u, c):
        for d in range(1, peers):
            plan_arrival(u, d).wait_recv()
        plan = pbuf[u, 0]
        for src in range(1, peers):
            plan = plan + pbuf[u, src]
        plan = plan / total_scen
        if sweep == SWEEPS - 1:
            plan_out[c] = plan
        for n in range(tiles):
            cols = slice(n * TILE, (n + 1) * TILE)
            now = st[c, :, :, cols]
            day = plan[:, cols]
            base = pr[c, :, :, cols]
            if sweep == 0:
                dual = now - day
                dd[c, :, :, cols] = dual
                pr[c, :, :, cols] = base + (0.5 * tie_weight) * mrow[:, cols] * now
            else:
                dual = dd[c, :, :, cols] + now - day
            kk[:, :, cols] = step_rate * (base + day_weight * (dual - day))
            rb[0, :, cols] = now.reshape(rows, TILE).astype(jnp.bfloat16)
        for n in range(tiles):
            cols = slice(n * TILE, (n + 1) * TILE)
            slope = jnp.dot(rb[0], mat[:, cols], preferred_element_type=jnp.float32).reshape(scens, SUB, TILE)
            first[:, :, cols] = arow[:, cols] * st[c, :, :, cols] - step_rate * slope - kk[:, :, cols]

    def descend(sweep, u, c, arrivals):
        top = arrivals[0][0]
        count = sum(span[1] for span in arrivals)
        lines = slice(top, top + count)
        some = slice(lines.start // SUB, lines.stop // SUB)
        for k in range(2):
            for span in arrivals:
                tie_copy(u, k, span).wait_recv()
            put_split(rcv[u, k, lines], k * slots, slots)

        def advance(n, new, step):
            cols = slice(n * TILE, (n + 1) * TILE)
            new = jnp.minimum(jnp.maximum(new, -dm[c, some, :, cols]), urow[:, cols])
            if step < STEPS - 1:
                rb[(step + 1) % 2, lines, cols] = new.reshape(count, TILE).astype(jnp.bfloat16)
            if sweep == SWEEPS - 1 and step == STEPS - 1:
                out[some, pl.ds(pl.multiple_of(c * SUB, SUB), SUB), cols] = new
            else:
                st[c, some, :, cols] = new

        for n in range(tiles):
            cols = slice(n * TILE, (n + 1) * TILE)
            theirs = select(place, n, count).reshape(count // SUB, SUB, TILE)
            if sweep == 0:
                pr[c, some, :, cols] -= (0.5 * tie_weight) * theirs
            pull = (step_rate * tie_weight) * theirs
            kk[some, :, cols] -= pull
            advance(n, first[some, :, cols] + pull, 0)
        for step in range(1, STEPS):
            for n in range(tiles):
                cols = slice(n * TILE, (n + 1) * TILE)
                slope = jnp.dot(rb[step % 2, lines], mat[:, cols], preferred_element_type=jnp.float32).reshape(count // SUB, SUB, TILE)
                advance(n, arow[:, cols] * st[c, some, :, cols] - step_rate * slope - kk[some, :, cols], step)

    @pl.loop(0, chunks)
    def first_sweep(c):
        load(1, price_hbm, pr, c).wait()
        load(2, demand_hbm, dm, c).wait()
        prepare(0, c, c)
        descend(0, c, c, (whole,))
        u = chunks + c
        pbuf[u, me] = jnp.sum(st[c] + dd[c], axis=0)
        send_plan(u)
        split_state(c)
        for k in range(2):
            gather_ties(u, k)

        @pl.when(c < chunks - 1)
        def _():
            send_ties(u, (whole,))

        @pl.when(c == chunks - 1)
        def _():
            send_ties(u, parts, (row, 1 - row) if square else (0, 1))

    @pl.loop(0, chunks - 1)
    def last_sweep(c):
        prepare(1, chunks + c, c)
        descend(1, chunks + c, c, (whole,))

    prepare(1, last, chunks - 1)
    for span in parts[:-1]:
        descend(1, last, chunks - 1, (span,))
    def finish(u):
        for d in range(1, peers):
            plan_copy(u, d).wait_send()

    pl.loop(0, SWEEPS * chunks)(finish)
    for k in range(2):
        pl.loop(0, last)(lambda u: tie_copy(u, k, whole).wait_send())
        for span in parts:
            tie_copy(last, k, span).wait_send()

    top, count = parts[-1]
    for k in range(2):
        tie_copy(last, k, parts[-1]).wait_recv()
        put_split(rcv[last, k, top:top + count], k * slots, slots)


def close(
    out, plan, dm, mat, place, arow, urow, split, kk, first,
    final_hbm, plan_hbm, st, kl, rb, sem,
):
    scens, hours, buses = out.shape
    tiles = buses // TILE
    some = slice(scens - scens // PARTS, scens)
    late = pl.ds(hours - SUB, SUB)
    count = (some.stop - some.start) * SUB
    early = (
        pltpu.make_async_copy(out.at[pl.ds(0, some.start)], final_hbm.at[pl.ds(0, some.start)], sem.at[0]),
        pltpu.make_async_copy(
            out.at[pl.ds(some.start, scens - some.start), pl.ds(0, hours - SUB)],
            final_hbm.at[pl.ds(some.start, scens - some.start), pl.ds(0, hours - SUB)], sem.at[1],
        ),
        pltpu.make_async_copy(plan, plan_hbm, sem.at[2]),
    )
    for copy in early:
        copy.start()
    last = dm.shape[0] - 1

    def advance(n, new, step):
        cols = slice(n * TILE, (n + 1) * TILE)
        new = jnp.minimum(jnp.maximum(new, -dm[last, some, :, cols]), urow[:, cols])
        if step < STEPS - 1:
            rb[step % 2, :, cols] = new.reshape(count, TILE).astype(jnp.bfloat16)
        st[:, :, cols] = new

    for n in range(tiles):
        cols = slice(n * TILE, (n + 1) * TILE)
        both = jnp.dot(split[:2 * count], place[:, cols], preferred_element_type=jnp.float32)
        pull = (step_rate * tie_weight) * (both[:count] + both[count:]).reshape(count // SUB, SUB, TILE)
        kl[:, :, cols] = kk[some, :, cols] - pull
        advance(n, first[some, :, cols] + pull, 0)
    for step in range(1, STEPS):
        for n in range(tiles):
            cols = slice(n * TILE, (n + 1) * TILE)
            slope = jnp.dot(rb[(step - 1) % 2], mat[:, cols], preferred_element_type=jnp.float32).reshape(count // SUB, SUB, TILE)
            advance(n, arow[:, cols] * st[:, :, cols] - step_rate * slope - kl[:, :, cols], step)
    end = pltpu.make_async_copy(st, final_hbm.at[pl.ds(some.start, scens - some.start), late], sem.at[3])
    end.start()
    for copy in early:
        copy.wait()
    end.wait()


def body(start_state, price, demand, sens, gen_bus, gen_cap, tie_index, tie_len):
    _, scens, hours, buses = start_state.shape
    slots = tie_index.shape[2]
    peers = lax.axis_size("scen")
    regions = lax.axis_size("region")
    chunks = hours // SUB
    rows = scens * SUB
    f32, bf16 = jnp.float32, jnp.bfloat16
    resident = pl.BlockSpec(memory_space=pltpu.VMEM)
    anywhere = pl.BlockSpec(memory_space=pl.ANY)
    whole = pltpu.VMEM((chunks, scens, SUB, buses), f32)
    made = pl.pallas_call(
        functools.partial(kernel, scens * peers, regions, peers),
        out_shape=(
            pltpu.VMEM((scens, hours, buses), f32),
            pltpu.VMEM((chunks, SUB, buses), f32),
            whole,
            pltpu.VMEM((buses, buses), bf16),
            pltpu.VMEM((2 * slots, buses), bf16),
            pltpu.VMEM((SUB, buses), f32),
            pltpu.VMEM((SUB, buses), f32),
            pltpu.VMEM((2 * rows, buses), bf16),
            pltpu.VMEM((scens, SUB, buses), f32),
            pltpu.VMEM((scens, SUB, buses), f32),
        ),
        in_specs=[pl.BlockSpec(memory_space=pltpu.HBM)] * 8,
        out_specs=(resident,) * 10,
        scratch_shapes=[
            pltpu.VMEM(gen_bus.shape, gen_bus.dtype),
            pltpu.VMEM(gen_cap.shape, gen_cap.dtype),
            pltpu.VMEM(tie_index.shape[1:], tie_index.dtype),
            pltpu.VMEM(tie_len.shape, tie_len.dtype),
            whole, whole, whole,
            pltpu.VMEM((buses, 2 * slots), bf16),
            pltpu.VMEM((SUB, buses), f32),
            pltpu.VMEM((2, rows, buses), bf16),
            pltpu.VMEM((SWEEPS * chunks, 2, rows, slots), f32),
            pltpu.VMEM((SWEEPS * chunks, 2, rows, slots), f32),
            pltpu.VMEM((SWEEPS * chunks, peers, SUB, buses), f32),
            pltpu.SemaphoreType.REGULAR((3,)),
            pltpu.SemaphoreType.DMA((4,)),
            pltpu.SemaphoreType.DMA((3, chunks - 1 + PARTS)),
            pltpu.SemaphoreType.DMA,
            pltpu.SemaphoreType.DMA((SWEEPS * chunks, 2, PARTS)),
            pltpu.SemaphoreType.DMA((SWEEPS * chunks, 2, PARTS)),
            pltpu.SemaphoreType.DMA((SWEEPS * chunks, peers)),
            pltpu.SemaphoreType.DMA((SWEEPS * chunks, peers)),
        ],
        compiler_params=pltpu.CompilerParams(collective_id=0, has_side_effects=True, vmem_limit_bytes=32 * 2**20),
        name="dispatch",
    )(*(
        pltpu.with_memory_space_constraint(one, pltpu.HBM)
        for one in (start_state[0], price[0], demand[0], sens[0], gen_bus, gen_cap, tie_index[0], tie_len)
    ))
    final, plan = pl.pallas_call(
        close,
        out_shape=(
            jax.ShapeDtypeStruct((scens, hours, buses), f32),
            jax.ShapeDtypeStruct((chunks, SUB, buses), f32),
        ),
        in_specs=[resident] * len(made),
        out_specs=(anywhere, anywhere),
        scratch_shapes=[
            pltpu.VMEM((scens // PARTS, SUB, buses), f32),
            pltpu.VMEM((scens // PARTS, SUB, buses), f32),
            pltpu.VMEM((2, rows // PARTS, buses), bf16),
            pltpu.SemaphoreType.DMA((4,)),
        ],
        compiler_params=pltpu.CompilerParams(vmem_limit_bytes=16 * 2**20),
        name="close",
    )(*(pltpu.with_memory_space_constraint(one, pltpu.VMEM) for one in made))
    return (final[None], plan.reshape(1, hours, buses))


def solution(mesh):
    in_specs = (
        P("region", "scen", None, None),
        P("region", "scen", None, None),
        P("region", "scen", None, None),
        P("region", None, None),
        P("region", None),
        P("region", None),
        P("region", None, None),
        P("region", None),
    )
    out_specs = (P("region", "scen", None, None), P("region", None, None))
    return jax.shard_map(body, mesh=mesh, in_specs=in_specs, out_specs=out_specs, check_vma=False)
```

```python
import functools
import jax
import jax.numpy as jnp
from jax import lax
from jax.experimental import pallas as pl
from jax.experimental.pallas import tpu as pltpu
from jax.sharding import PartitionSpec as P

SWEEPS = 2
STEPS = 3
SUB = 8
LANES = 128
TILE = 256
PARTS = 2


step_rate = 0.3
tie_weight = 1.0
day_weight = 0.5

MESH = pl.DeviceIdType.MESH


def kernel(
    total_scen, regions, peers,
    s0_hbm, price_hbm, demand_hbm, sens_hbm, gen_bus_hbm, gen_cap_hbm, tie_index_hbm, tie_len_hbm,
    out, plan_out, dm, mat, place, arow, urow, split, kk, first,
    gen_bus, gen_cap, tie_index, tie_len,
    st, dd, pr, pick, mrow, rb,
    snd, rcv, pbuf,
    token, small_sem, in_sem, mat_sem, send_sem, recv_sem, psend_sem, precv_sem,
):
    chunks, scens, _, buses = st.shape
    slots = tie_index.shape[1]
    rows = scens * SUB
    tiles = buses // TILE
    me = lax.axis_index("scen")
    reg = lax.axis_index("region")
    odd = lax.rem(reg, 2)
    near = reg + 1 - 2 * odd
    far = lax.rem(reg + regions - 1 + 2 * odd, regions)
    square = regions == 4
    across = lax.rem(reg + 2, regions)
    row = lax.div(reg, 2)
    part_rows = rows // PARTS
    part_scens = scens // PARTS
    whole = (0, rows)
    parts = tuple((part * part_rows, part_rows) for part in range(PARTS))
    last = SWEEPS * chunks - 1

    def load(kind, source, target, c):
        return pltpu.make_async_copy(source.at[:, pl.ds(pl.multiple_of(c * SUB, SUB), SUB), :], target.at[c], in_sem.at[kind, c])

    def load_first(part):
        some = pl.ds(part * part_scens, part_scens)
        return pltpu.make_async_copy(s0_hbm.at[some, pl.ds(0, SUB), :], st.at[0, some], in_sem.at[0, 0 if part == 0 else chunks - 1 + part])

    small = [
        pltpu.make_async_copy(source, target, small_sem.at[i])
        for i, (source, target) in enumerate((
            (tie_index_hbm, tie_index), (tie_len_hbm, tie_len), (gen_bus_hbm, gen_bus), (gen_cap_hbm, gen_cap),
        ))
    ]
    small[0].start()
    load_first(0).start()

    barrier = pltpu.get_barrier_semaphore()
    pl.semaphore_signal(barrier, inc=1, device_id={"region": near}, device_id_type=MESH)

    @pl.when((row == 0) if square else True)
    def _():
        pl.semaphore_signal(barrier, inc=1, device_id={"region": across if square else far}, device_id_type=MESH)

    half = lax.rem(me, 2)
    place_z = lax.div(me, 2)
    last_z = peers // 2 - 1
    lower, higher = {"scen": me - 2}, {"scen": me + 2}
    pl.semaphore_signal(barrier, inc=1, device_id={"scen": me + 1 - 2 * half}, device_id_type=MESH)

    @pl.when(place_z > 0)
    def _():
        pl.semaphore_signal(barrier, inc=1, device_id=lower, device_id_type=MESH)

    @pl.when(place_z < last_z)
    def _():
        pl.semaphore_signal(barrier, inc=1, device_id=higher, device_id_type=MESH)

    for part in range(1, PARTS):
        load_first(part).start()
    for c in range(1, chunks):
        load(0, s0_hbm, st, c).start()
    for copy in small[1:]:
        copy.start()

    mat_copy = pltpu.make_async_copy(sens_hbm, mat, mat_sem)

    def one_hot(hit):
        return jnp.where(hit, 1.0, 0.0)

    def side(k):
        return 1 - odd if k == 0 else odd

    def tie_row(k):
        return tie_index[pl.ds(side(k), 1), :]

    def build_pick(k, at):
        lanes = slice(at * TILE, (at + 1) * TILE)
        wanted = jnp.broadcast_to(tie_row(k)[:, lanes], (LANES, TILE))
        for b in range(buses // LANES):
            ids = lax.broadcasted_iota(jnp.int32, (LANES, TILE), 0) + b * LANES
            pick[b * LANES:(b + 1) * LANES, k * slots + at * TILE:k * slots + (at + 1) * TILE] = one_hot(ids == wanted).astype(jnp.bfloat16)

    small[0].wait()
    build_pick(0, 0)

    def tie_copy(u, k, span, lanes=slice(None)):
        part = span[0] // part_rows
        block = pl.ds(*span)
        return pltpu.make_async_remote_copy(
            src_ref=snd.at[u, k, block, lanes], dst_ref=rcv.at[u, k, block, lanes],
            send_sem=send_sem.at[u, k, part], recv_sem=recv_sem.at[u, k, part],
            device_id={"region": jnp.where(k == 0, near, far)}, device_id_type=MESH,
        )

    def plan_copy(u, d):
        return pltpu.make_async_remote_copy(
            src_ref=pbuf.at[u, me], dst_ref=pbuf.at[u, me],
            send_sem=psend_sem.at[u, d], recv_sem=precv_sem.at[u, me],
            device_id={"scen": lax.rem(me + d, peers)}, device_id_type=MESH,
        )

    def plan_arrival(u, d):
        src = lax.rem(me + d, peers)
        return pltpu.make_async_remote_copy(
            src_ref=pbuf.at[u, src], dst_ref=pbuf.at[u, src],
            send_sem=psend_sem.at[u, d], recv_sem=precv_sem.at[u, src],
            device_id={"scen": src}, device_id_type=MESH,
        )

    def put_split(value, at, width):
        count = value.shape[0]
        high = value.astype(jnp.bfloat16)
        split[:count, at:at + width] = high
        split[count:2 * count, at:at + width] = (value - high.astype(jnp.float32)).astype(jnp.bfloat16)

    def select(weights, n, count):
        both = jnp.dot(split[:2 * count], weights[:, n * TILE:(n + 1) * TILE], preferred_element_type=jnp.float32)
        return both[:count] + both[count:]

    per_side = slots // TILE

    def split_state(c):
        for n in range(tiles):
            put_split(st[c, :, :, n * TILE:(n + 1) * TILE].reshape(rows, TILE), n * TILE, TILE)

    def gather_ties(u, k):
        for at in range(per_side):
            snd[u, k, :, at * TILE:(at + 1) * TILE] = select(pick, k * per_side + at, rows)

    def send_ties(u, spans, sides=(0, 1)):
        for k in sides:
            for span in spans:
                tie_copy(u, k, span).start()

    def send_plan(u):
        for d in range(1, peers):
            plan_copy(u, d).start()

    def enter():
        pl.semaphore_wait(barrier, (2 + row if square else 3) + lax.div(place_z + last_z, last_z + 1) + lax.div(2 * last_z - place_z, last_z + 1))

    def greet_far():
        @pl.when(place_z == last_z)
        def _():
            pl.semaphore_signal(token.at[1], inc=1, device_id=lower, device_id_type=MESH)

        @pl.when(place_z > 0)
        def _():
            pl.semaphore_wait(token.at[0], 1)

        @pl.when(place_z < last_z)
        def _():
            pl.semaphore_signal(token.at[0], inc=1, device_id=higher, device_id_type=MESH)
            pl.semaphore_wait(token.at[1], 1)

        @pl.when((place_z > 0) & (place_z < last_z))
        def _():
            pl.semaphore_signal(token.at[1], inc=1, device_id=lower, device_id_type=MESH)

    def start_first():
        for part in range(PARTS):
            load_first(part).wait()
            some = slice(part * part_scens, (part + 1) * part_scens)
            base = part * 2 * part_rows
            for n in range(tiles):
                cols = slice(n * TILE, (n + 1) * TILE)
                value = st[0, some, :, cols].reshape(part_rows, TILE)
                high = value.astype(jnp.bfloat16)
                split[base:base + part_rows, cols] = high
                split[base + part_rows:base + 2 * part_rows, cols] = (value - high.astype(jnp.float32)).astype(jnp.bfloat16)
            for at in range(per_side):
                if part == 0 and at > 0:
                    build_pick(0, at)
                gather_first(0, part, at)
                if part == 0 and at == 0:
                    enter()
                    if square:
                        @pl.when(row == 1)
                        def _():
                            pl.semaphore_signal(token.at[3], inc=1, device_id={"region": across}, device_id_type=MESH)
                            pl.semaphore_signal(token.at[2], inc=1, device_id={"region": near}, device_id_type=MESH)
                first_copy(part, at).start()
        if square:
            @pl.when(row == 0)
            def _():
                pl.semaphore_wait(token.at[3], 1)
                pl.semaphore_signal(token.at[2], inc=1, device_id={"region": near}, device_id_type=MESH)

        for at in range(per_side):
            build_pick(1, at)
            for part in range(PARTS):
                gather_first(1, part, at)
        if square:
            pl.semaphore_wait(token.at[2], 1)
        tie_copy(0, 1, whole).start()
        mat_copy.start()
        for c in range(chunks):
            load(1, price_hbm, pr, c).start()
            load(2, demand_hbm, dm, c).start()
        pbuf[0, me] = jnp.sum(st[0], axis=0)

    def first_copy(part, at):
        block = pl.ds(part * part_rows, part_rows)
        lanes = pl.ds(at * TILE, TILE)
        return pltpu.make_async_remote_copy(
            src_ref=snd.at[0, 0, block, lanes], dst_ref=rcv.at[0, 0, block, lanes],
            send_sem=send_sem.at[0, 0, 0], recv_sem=recv_sem.at[0, 0, 0],
            device_id={"region": near}, device_id_type=MESH,
        )

    def gather_first(k, part, at):
        base = part * 2 * part_rows
        n = k * per_side + at
        both = jnp.dot(split[base:base + 2 * part_rows], pick[:, n * TILE:(n + 1) * TILE], preferred_element_type=jnp.float32)
        snd[0, k, part * part_rows:(part + 1) * part_rows, at * TILE:(at + 1) * TILE] = both[:part_rows] + both[part_rows:]

    def start_chunk(c):
        load(0, s0_hbm, st, c).wait()
        split_state(c)
        for k in range(2):
            gather_ties(c, k)
            tie_copy(c, k, whole).start()
        pbuf[c, me] = jnp.sum(st[c], axis=0)

    start_first()
    pl.loop(1, chunks)(start_chunk)

    for copy in small[1:]:
        copy.wait()
    for k in range(2):
        column = jnp.transpose(jnp.broadcast_to(tie_row(k).astype(jnp.float32), (LANES, slots))).astype(jnp.int32)
        limit = jnp.where(side(k) == 0, tie_len[0:1, 0:1], tie_len[0:1, 1:2])
        alive = lax.broadcasted_iota(jnp.int32, (slots, LANES), 0) < limit
        for b in range(buses // LANES):
            ids = lax.broadcasted_iota(jnp.int32, (slots, LANES), 1) + b * LANES
            hot = one_hot((ids == column) & alive)
            place[k * slots:(k + 1) * slots, b * LANES:(b + 1) * LANES] = hot.astype(jnp.bfloat16)
            part = jnp.broadcast_to(jnp.sum(hot, axis=0, keepdims=True), (SUB, LANES))
            if k == 0:
                mrow[:, b * LANES:(b + 1) * LANES] = part
            else:
                mrow[:, b * LANES:(b + 1) * LANES] += part
    arow[...] = 1.0 - step_rate * (tie_weight * mrow[...] + day_weight)
    gens = gen_bus.shape[1]
    column = jnp.transpose(jnp.broadcast_to(gen_bus[...].astype(jnp.float32), (LANES, gens))).astype(jnp.int32)
    caps = jnp.transpose(jnp.broadcast_to(gen_cap[...], (LANES, gens)))
    for b in range(buses // LANES):
        ids = lax.broadcasted_iota(jnp.int32, (gens, LANES), 1) + b * LANES
        part = jnp.sum(jnp.where(ids == column, caps, 0.0), axis=0, keepdims=True)
        urow[:, b * LANES:(b + 1) * LANES] = jnp.broadcast_to(part, (SUB, LANES))
    greet_far()
    pl.loop(0, chunks)(send_plan)
    mat_copy.wait()

    def prepare(sweep, u, c):
        for d in range(1, peers):
            plan_arrival(u, d).wait_recv()
        plan = pbuf[u, 0]
        for src in range(1, peers):
            plan = plan + pbuf[u, src]
        plan = plan / total_scen
        if sweep == SWEEPS - 1:
            plan_out[c] = plan
        for n in range(tiles):
            cols = slice(n * TILE, (n + 1) * TILE)
            now = st[c, :, :, cols]
            day = plan[:, cols]
            base = pr[c, :, :, cols]
            if sweep == 0:
                dual = now - day
                dd[c, :, :, cols] = dual
                pr[c, :, :, cols] = base + (0.5 * tie_weight) * mrow[:, cols] * now
            else:
                dual = dd[c, :, :, cols] + now - day
            kk[:, :, cols] = step_rate * (base + day_weight * (dual - day))
            rb[0, :, cols] = now.reshape(rows, TILE).astype(jnp.bfloat16)
        for n in range(tiles):
            cols = slice(n * TILE, (n + 1) * TILE)
            slope = jnp.dot(rb[0], mat[:, cols], preferred_element_type=jnp.float32).reshape(scens, SUB, TILE)
            first[:, :, cols] = arow[:, cols] * st[c, :, :, cols] - step_rate * slope - kk[:, :, cols]

    def descend(sweep, u, c, arrivals):
        top = arrivals[0][0]
        count = sum(span[1] for span in arrivals)
        lines = slice(top, top + count)
        some = slice(lines.start // SUB, lines.stop // SUB)
        for k in range(2):
            for span in arrivals:
                tie_copy(u, k, span).wait_recv()
            put_split(rcv[u, k, lines], k * slots, slots)

        def advance(n, new, step):
            cols = slice(n * TILE, (n + 1) * TILE)
            new = jnp.minimum(jnp.maximum(new, -dm[c, some, :, cols]), urow[:, cols])
            if step < STEPS - 1:
                rb[(step + 1) % 2, lines, cols] = new.reshape(count, TILE).astype(jnp.bfloat16)
            if sweep == SWEEPS - 1 and step == STEPS - 1:
                out[some, pl.ds(pl.multiple_of(c * SUB, SUB), SUB), cols] = new
            else:
                st[c, some, :, cols] = new

        for n in range(tiles):
            cols = slice(n * TILE, (n + 1) * TILE)
            theirs = select(place, n, count).reshape(count // SUB, SUB, TILE)
            if sweep == 0:
                pr[c, some, :, cols] -= (0.5 * tie_weight) * theirs
            pull = (step_rate * tie_weight) * theirs
            kk[some, :, cols] -= pull
            advance(n, first[some, :, cols] + pull, 0)
        for step in range(1, STEPS):
            for n in range(tiles):
                cols = slice(n * TILE, (n + 1) * TILE)
                slope = jnp.dot(rb[step % 2, lines], mat[:, cols], preferred_element_type=jnp.float32).reshape(count // SUB, SUB, TILE)
                advance(n, arow[:, cols] * st[c, some, :, cols] - step_rate * slope - kk[some, :, cols], step)

    @pl.loop(0, chunks)
    def first_sweep(c):
        load(1, price_hbm, pr, c).wait()
        load(2, demand_hbm, dm, c).wait()
        prepare(0, c, c)
        descend(0, c, c, (whole,))
        u = chunks + c
        pbuf[u, me] = jnp.sum(st[c] + dd[c], axis=0)
        send_plan(u)
        split_state(c)
        for k in range(2):
            gather_ties(u, k)

        @pl.when(c < chunks - 1)
        def _():
            send_ties(u, (whole,))

        @pl.when(c == chunks - 1)
        def _():
            send_ties(u, parts, (row, 1 - row) if square else (0, 1))

    @pl.loop(0, chunks - 1)
    def last_sweep(c):
        prepare(1, chunks + c, c)
        descend(1, chunks + c, c, (whole,))

    prepare(1, last, chunks - 1)
    for span in parts[:-1]:
        descend(1, last, chunks - 1, (span,))
    def finish(u):
        for d in range(1, peers):
            plan_copy(u, d).wait_send()

    pl.loop(0, SWEEPS * chunks)(finish)
    for k in range(2):
        pl.loop(0, last)(lambda u: tie_copy(u, k, whole).wait_send())
        for span in parts:
            tie_copy(last, k, span).wait_send()

    top, count = parts[-1]
    for k in range(2):
        tie_copy(last, k, parts[-1]).wait_recv()
        put_split(rcv[last, k, top:top + count], k * slots, slots)


def close(
    out, plan, dm, mat, place, arow, urow, split, kk, first,
    final_hbm, plan_hbm, st, kl, rb, sem,
):
    scens, hours, buses = out.shape
    tiles = buses // TILE
    some = slice(scens - scens // PARTS, scens)
    late = pl.ds(hours - SUB, SUB)
    count = (some.stop - some.start) * SUB
    early = (
        pltpu.make_async_copy(out.at[pl.ds(0, some.start)], final_hbm.at[pl.ds(0, some.start)], sem.at[0]),
        pltpu.make_async_copy(
            out.at[pl.ds(some.start, scens - some.start), pl.ds(0, hours - SUB)],
            final_hbm.at[pl.ds(some.start, scens - some.start), pl.ds(0, hours - SUB)], sem.at[1],
        ),
        pltpu.make_async_copy(plan, plan_hbm, sem.at[2]),
    )
    for copy in early:
        copy.start()
    last = dm.shape[0] - 1

    def advance(n, new, step):
        cols = slice(n * TILE, (n + 1) * TILE)
        new = jnp.minimum(jnp.maximum(new, -dm[last, some, :, cols]), urow[:, cols])
        if step < STEPS - 1:
            rb[step % 2, :, cols] = new.reshape(count, TILE).astype(jnp.bfloat16)
        st[:, :, cols] = new

    for n in range(tiles):
        cols = slice(n * TILE, (n + 1) * TILE)
        both = jnp.dot(split[:2 * count], place[:, cols], preferred_element_type=jnp.float32)
        pull = (step_rate * tie_weight) * (both[:count] + both[count:]).reshape(count // SUB, SUB, TILE)
        kl[:, :, cols] = kk[some, :, cols] - pull
        advance(n, first[some, :, cols] + pull, 0)
    for step in range(1, STEPS):
        for n in range(tiles):
            cols = slice(n * TILE, (n + 1) * TILE)
            slope = jnp.dot(rb[(step - 1) % 2], mat[:, cols], preferred_element_type=jnp.float32).reshape(count // SUB, SUB, TILE)
            advance(n, arow[:, cols] * st[:, :, cols] - step_rate * slope - kl[:, :, cols], step)
    end = pltpu.make_async_copy(st, final_hbm.at[pl.ds(some.start, scens - some.start), late], sem.at[3])
    end.start()
    for copy in early:
        copy.wait()
    end.wait()


def body(start_state, price, demand, sens, gen_bus, gen_cap, tie_index, tie_len):
    _, scens, hours, buses = start_state.shape
    slots = tie_index.shape[2]
    peers = lax.axis_size("scen")
    regions = lax.axis_size("region")
    chunks = hours // SUB
    rows = scens * SUB
    f32, bf16 = jnp.float32, jnp.bfloat16
    resident = pl.BlockSpec(memory_space=pltpu.VMEM)
    anywhere = pl.BlockSpec(memory_space=pl.ANY)
    whole = pltpu.VMEM((chunks, scens, SUB, buses), f32)
    made = pl.pallas_call(
        functools.partial(kernel, scens * peers, regions, peers),
        out_shape=(
            pltpu.VMEM((scens, hours, buses), f32),
            pltpu.VMEM((chunks, SUB, buses), f32),
            whole,
            pltpu.VMEM((buses, buses), bf16),
            pltpu.VMEM((2 * slots, buses), bf16),
            pltpu.VMEM((SUB, buses), f32),
            pltpu.VMEM((SUB, buses), f32),
            pltpu.VMEM((2 * rows, buses), bf16),
            pltpu.VMEM((scens, SUB, buses), f32),
            pltpu.VMEM((scens, SUB, buses), f32),
        ),
        in_specs=[pl.BlockSpec(memory_space=pltpu.HBM)] * 8,
        out_specs=(resident,) * 10,
        scratch_shapes=[
            pltpu.VMEM(gen_bus.shape, gen_bus.dtype),
            pltpu.VMEM(gen_cap.shape, gen_cap.dtype),
            pltpu.VMEM(tie_index.shape[1:], tie_index.dtype),
            pltpu.VMEM(tie_len.shape, tie_len.dtype),
            whole, whole, whole,
            pltpu.VMEM((buses, 2 * slots), bf16),
            pltpu.VMEM((SUB, buses), f32),
            pltpu.VMEM((2, rows, buses), bf16),
            pltpu.VMEM((SWEEPS * chunks, 2, rows, slots), f32),
            pltpu.VMEM((SWEEPS * chunks, 2, rows, slots), f32),
            pltpu.VMEM((SWEEPS * chunks, peers, SUB, buses), f32),
            pltpu.SemaphoreType.REGULAR((4,)),
            pltpu.SemaphoreType.DMA((4,)),
            pltpu.SemaphoreType.DMA((3, chunks - 1 + PARTS)),
            pltpu.SemaphoreType.DMA,
            pltpu.SemaphoreType.DMA((SWEEPS * chunks, 2, PARTS)),
            pltpu.SemaphoreType.DMA((SWEEPS * chunks, 2, PARTS)),
            pltpu.SemaphoreType.DMA((SWEEPS * chunks, peers)),
            pltpu.SemaphoreType.DMA((SWEEPS * chunks, peers)),
        ],
        compiler_params=pltpu.CompilerParams(collective_id=0, has_side_effects=True, vmem_limit_bytes=32 * 2**20),
        name="dispatch",
    )(*(
        pltpu.with_memory_space_constraint(one, pltpu.HBM)
        for one in (start_state[0], price[0], demand[0], sens[0], gen_bus, gen_cap, tie_index[0], tie_len)
    ))
    final, plan = pl.pallas_call(
        close,
        out_shape=(
            jax.ShapeDtypeStruct((scens, hours, buses), f32),
            jax.ShapeDtypeStruct((chunks, SUB, buses), f32),
        ),
        in_specs=[resident] * len(made),
        out_specs=(anywhere, anywhere),
        scratch_shapes=[
            pltpu.VMEM((scens // PARTS, SUB, buses), f32),
            pltpu.VMEM((scens // PARTS, SUB, buses), f32),
            pltpu.VMEM((2, rows // PARTS, buses), bf16),
            pltpu.SemaphoreType.DMA((4,)),
        ],
        compiler_params=pltpu.CompilerParams(vmem_limit_bytes=16 * 2**20),
        name="close",
    )(*(pltpu.with_memory_space_constraint(one, pltpu.VMEM) for one in made))
    return (final[None], plan.reshape(1, hours, buses))


def solution(mesh):
    in_specs = (
        P("region", "scen", None, None),
        P("region", "scen", None, None),
        P("region", "scen", None, None),
        P("region", None, None),
        P("region", None),
        P("region", None),
        P("region", None, None),
        P("region", None),
    )
    out_specs = (P("region", "scen", None, None), P("region", None, None))
    return jax.shard_map(body, mesh=mesh, in_specs=in_specs, out_specs=out_specs, check_vma=False)
```
